32 devices in a mesh: ctx: 8 (over z, y), fsdp: 4 (over x, core).
Axes of the slice: x: 2, y: 2, z: 4, core: 2. Of those that a mesh axis runs over, the one named last changes fastest.
Arguments:
- tokens: bfloat16 [4, 1024, 2048], P('fsdp', 'ctx'), may hold values from -6 to 6
- layer_input: bfloat16 [4, 1024, 256], P('fsdp', 'ctx'), may hold values from -6 to 6
- cotangent: bfloat16 [4, 1024, 2048], P('fsdp', 'ctx'), may hold values from -6 to 6
- doc_lengths: int32 [4, 4], P('fsdp'), may hold values from 1 to 512, 1024 in all within a row
- pair_of: int32 [8], replicated, may hold values from 0 to 7, each once
- w_query: float32 [2048, 2048], P(('ctx', 'fsdp')), may hold values from -0.125 to 0.125
- w_key: float32 [2048, 512], P(('ctx', 'fsdp')), may hold values from -0.125 to 0.125
- w_value: float32 [2048, 512], P(('ctx', 'fsdp')), may hold values from -0.125 to 0.125
- w_out: float32 [2048, 2048], P(('ctx', 'fsdp')), may hold values from -0.125 to 0.125
- w_left: float32 [2048, 64], P(('ctx', 'fsdp')), may hold values from -0.125 to 0.125
- w_right: float32 [64, 2048], P(None, ('ctx', 'fsdp')), may hold values from -0.75 to 0.75
- norm_gains: float32 [6, 2048], P(None, ('ctx', 'fsdp')), may hold values from 0.5 to 1.5
- qk_gain: float32 [2, 256], P(None, ('ctx', 'fsdp')), may hold values from 0.25 to 0.5
- w_gate: float32 [2048, 8192], P(('ctx', 'fsdp')), may hold values from -0.125 to 0.125
- w_up: float32 [2048, 8192], P(('ctx', 'fsdp')), may hold values from -0.125 to 0.125
- w_down: float32 [8192, 2048], P(('ctx', 'fsdp')), may hold values from -0.0625 to 0.0625
- w_pgate: float32 [2048, 256], P(('ctx', 'fsdp')), may hold values from -0.125 to 0.125
- w_pproj: float32 [256, 2048], P(None, ('ctx', 'fsdp')), may hold values from -0.375 to 0.375
Outputs:
- output: bfloat16 [4, 1024, 2048], P('fsdp', 'ctx')
- d_tokens: bfloat16 [4, 1024, 2048], P('fsdp', 'ctx')
- d_layer_input: bfloat16 [4, 1024, 256], P('fsdp', 'ctx')
- grad_query: float32 [2048, 2048], P(('ctx', 'fsdp'))
- grad_key: float32 [2048, 512], P(('ctx', 'fsdp'))
- grad_value: float32 [2048, 512], P(('ctx', 'fsdp'))
- grad_out: float32 [2048, 2048], P(('ctx', 'fsdp'))
- grad_left: float32 [2048, 64], P(('ctx', 'fsdp'))
- grad_right: float32 [64, 2048], P(None, ('ctx', 'fsdp'))
- grad_gains: float32 [6, 2048], P(None, ('ctx', 'fsdp'))
- grad_qk: float32 [2, 256], P(None, ('ctx', 'fsdp'))
- grad_gate: float32 [2048, 8192], P(('ctx', 'fsdp'))
- grad_up: float32 [2048, 8192], P(('ctx', 'fsdp'))
- grad_down: float32 [8192, 2048], P(('ctx', 'fsdp'))
- grad_pgate: float32 [2048, 256], P(('ctx', 'fsdp'))
- grad_pproj: float32 [256, 2048], P(None, ('ctx', 'fsdp'))
The draws below stay inside these ranges and needn't reach their ends.
Inputs may be any that keep to these rules, and one draw needn't show every extreme that they name: `doc_lengths`: each row sums to 1024; its longest document has exactly 512 tokens. A permutation: index c of ctx holds, in this order, blocks pair_of[c] and 15 - pair_of[c] of 64 tokens of its stream.
All inputs are finite; a program needn't handle non-finite values.
Results may differ from the reference program's by a relative error of at most 0.02.
The reference program's roundings to bfloat16 on the way count: a program that leaves them out, or rounds other values in their place, can miss the bound.
Values may be sent and summed in bfloat16 or wider, within the bound.
No kernel may reach another device: no remote copies, remote signals or barrier semaphores. Data moves between devices by JAX's collectives and lax.ppermute only.
A program may use at most 448 MiB of HBM per device.

```python
import math
import jax
import jax.numpy as jnp
import numpy as np
from jax import lax

D = 2048
H = 8
KVH = 2
HD = 256
FF = 8192
LR = 64
PLE = 256
TOK_DEV = 128
STREAMS = 4
SEQ = 1024
DOC_MAX = 512
NDOC = 4
N_CTX = 8


def level_of(rng, shape, shards, low, top_value):
    level = 1.0
    for dim, shards_of in shards:
        heights = jax.random.uniform(jax.random.fold_in(jax.random.fold_in(rng, 6), dim), (shards_of,), jnp.float32, low / len(shards), top_value / len(shards))
        level = level * jnp.repeat(jnp.exp(heights), shape[dim] // shards_of).reshape((-1,) + (1,) * (len(shape) - 1 - dim))
    return level


def profile(amount, total, limit, slope):
    loads = [(1 << 20) // math.isqrt(rank ** slope) + 1 for rank in range(2, amount + 1)]
    surplus, holding = total - limit - (amount - 1), [1] * (amount - 1)
    while surplus > 0:
        movable = [i for i in range(amount - 1) if holding[i] < limit]
        mass, left = sum([loads[i] for i in movable]), surplus
        for i in movable:
            more = min(limit - holding[i], max(1, left * loads[i] // mass), surplus)
            holding[i] = holding[i] + more
            surplus = surplus - more
    return np.array([limit] + holding)


def uneven(stream_key, count, total, bound, skew):
    if count == 2:
        one = jax.random.randint(stream_key, (), max(1, total - bound), min(bound, total - 1) + 1)
        return jnp.stack([one, total - one])
    tallies = jnp.asarray(profile(count, total, bound, skew), jnp.int32)
    twos = (count - 1) // 2
    giver, sink = tallies[1:1 + 2 * twos:2], tallies[2:2 + 2 * twos:2]
    margin = jnp.minimum(giver - 1, bound - sink)
    shifted = jax.random.randint(jax.random.fold_in(stream_key, 1), (twos,), 0, 1 << 20) % (margin + 1)
    tallies = tallies.at[1:1 + 2 * twos:2].set(giver - shifted).at[2:2 + 2 * twos:2].set(sink + shifted)
    return tallies[jax.random.permutation(jax.random.fold_in(stream_key, 2), count)]


def gaussian(stream_key, dims, spread, most, cuts=(), kind=jnp.bfloat16):
    entries = spread * jax.random.normal(stream_key, dims, jnp.float32)
    if cuts:
        entries = entries * level_of(stream_key, dims, cuts, -0.22, 0.18)
    return jnp.clip(entries, -most, most).astype(kind)


def setup_inputs(seed: int = 0) -> dict:
    key_list = jax.random.split(jax.random.key(seed), 19)
    tokens = gaussian(key_list[0], (STREAMS, SEQ, D), 1.0, 6.0, ((0, 4), (1, 8)))
    layer_input = gaussian(key_list[1], (STREAMS, SEQ, PLE), 1.0, 6.0, ((0, 4), (1, 8)))
    cotangent = gaussian(key_list[2], (STREAMS, SEQ, D), 1.0, 6.0, ((0, 4), (1, 8)))
    doc_lengths = jax.vmap(lambda own: uneven(own, NDOC, SEQ, DOC_MAX, 2))(jax.random.split(key_list[3], STREAMS)).reshape((STREAMS, NDOC)).astype(jnp.int32)
    pair_of = jax.random.permutation(key_list[4], N_CTX).astype(jnp.int32)
    w_query = gaussian(key_list[5], (D, H * HD), D ** -0.5, 0.125, ((0, 32),), jnp.float32)
    w_key = gaussian(key_list[6], (D, KVH * HD), D ** -0.5, 0.125, ((0, 32),), jnp.float32)
    w_value = gaussian(key_list[7], (D, KVH * HD), D ** -0.5, 0.125, ((0, 32),), jnp.float32)
    w_out = gaussian(key_list[8], (H * HD, D), (H * HD) ** -0.5, 0.125, ((0, 32),), jnp.float32)
    w_left = gaussian(key_list[9], (D, LR), D ** -0.5, 0.125, ((0, 32),), jnp.float32)
    w_right = gaussian(key_list[10], (LR, D), LR ** -0.5, 0.75, ((1, 32),), jnp.float32)
    norm_gains = jnp.clip(1.0 + 0.1 * jax.random.normal(key_list[11], (6, D), jnp.float32), 0.5, 1.5)
    qk_gain = jnp.clip(jnp.exp(math.log(0.5) - 0.6931472 * jax.random.uniform(key_list[12], (2, HD), jnp.float32) ** level_of(key_list[12], (2, HD), ((1, 32),), -0.2, 0.2)), 0.25, 0.5)
    w_gate = gaussian(key_list[13], (D, FF), D ** -0.5, 0.125, ((0, 32),), jnp.float32)
    w_up = gaussian(key_list[14], (D, FF), D ** -0.5, 0.125, ((0, 32),), jnp.float32)
    w_down = gaussian(key_list[15], (FF, D), FF ** -0.5, 0.0625, ((0, 32),), jnp.float32)
    w_pgate = gaussian(key_list[16], (D, PLE), D ** -0.5, 0.125, ((0, 32),), jnp.float32)
    w_pproj = gaussian(key_list[17], (PLE, D), PLE ** -0.5, 0.375, ((1, 32),), jnp.float32)
    return {"tokens": tokens, "layer_input": layer_input, "cotangent": cotangent, "doc_lengths": doc_lengths, "pair_of": pair_of, "w_query": w_query, "w_key": w_key, "w_value": w_value, "w_out": w_out, "w_left": w_left, "w_right": w_right, "norm_gains": norm_gains, "qk_gain": qk_gain, "w_gate": w_gate, "w_up": w_up, "w_down": w_down, "w_pgate": w_pgate, "w_pproj": w_pproj}


EPSILON = 1e-06
ROPE_BASE = 1000000.0
HALF_ROOT = 0.7071067811865476
MASKED = -1e+30
HIGHEST = lax.Precision.HIGHEST

@jax.custom_vjp
def low(v):
    return lax.optimization_barrier(v.astype(jnp.bfloat16)).astype(jnp.float32)

@jax.custom_vjp
def low_back(v):
    return v

def low_keep(v):
    return (low(v), None)

def low_pass(kept, grad):
    return (grad,)

def back_keep(v):
    return (v, None)

def back_low(kept, grad):
    return (low(grad),)
low.defvjp(low_keep, low_pass)
low_back.defvjp(back_keep, back_low)

def rms_norm(values_in, gain_in):
    return values_in * lax.rsqrt(lax.optimization_barrier(jnp.mean(values_in * values_in, axis=-1, keepdims=True)) + EPSILON) * gain_in

def gelu_tanh(values_in):
    return jax.nn.gelu(values_in, approximate=True)

def tables(rel_pos, head_size):
    frequency = ROPE_BASE ** (-2.0 * jnp.arange(head_size // 2, dtype=jnp.float32) / head_size)
    angles = rel_pos.astype(jnp.float32)[:, None] * frequency[None, :]
    return (jnp.cos(angles)[:, None, :], jnp.sin(angles)[:, None, :])

def rotate(values_in, cos_tab, sine_tab):
    half_width = values_in.shape[-1] // 2
    first_half = values_in[..., :half_width]
    second_half = values_in[..., half_width:]
    return jnp.concatenate([first_half * cos_tab - second_half * sine_tab, second_half * cos_tab + first_half * sine_tab], axis=-1)

def layout(pair_of, lengths, row_count):
    dev_count = pair_of.shape[0]
    local_row = jnp.arange(row_count * dev_count, dtype=jnp.int32) % row_count
    half_rows = row_count // 2
    pair_idx = jnp.repeat(pair_of.astype(jnp.int32), row_count)
    block_idx = jnp.where(local_row < half_rows, pair_idx, 2 * dev_count - 1 - pair_idx)
    position = block_idx * half_rows + local_row % half_rows
    doc_lens = lengths.astype(jnp.int32)
    doc_ends = jnp.cumsum(doc_lens, dtype=jnp.int32)
    before = doc_ends[None, :] <= position[:, None]
    segment = lax.optimization_barrier(jnp.sum(before.astype(jnp.int32), axis=1, dtype=jnp.int32))
    doc_start = lax.optimization_barrier(jnp.sum(jnp.where(before, doc_lens[None, :], 0), axis=1, dtype=jnp.int32))
    return (position, segment, position - doc_start)

def matmul_hi(left_in, right_in):
    return jnp.dot(left_in, right_in, precision=HIGHEST, preferred_element_type=jnp.float32)

def attend(query_rows, key_rows, value_rows, position, segment):
    seq_len = query_rows.shape[0]
    block_count = seq_len // TOK_DEV

    def per_block(block_args):
        query_blk, pos_blk, seg_blk = block_args
        scores = low_back(jnp.einsum('rkgd,skd->kgrs', query_blk, key_rows, precision=HIGHEST))
        visible = (segment[None, :] == seg_blk[:, None]) & (position[None, :] <= pos_blk[:, None])
        scores = jnp.where(visible[None, None], scores, MASKED)
        top_score = lax.optimization_barrier(jnp.max(scores, axis=-1, keepdims=True))
        log_total = top_score + jnp.log(lax.optimization_barrier(jnp.sum(jnp.exp(scores - top_score), axis=-1, keepdims=True)))
        prob_low = low(jnp.exp(scores - log_total))
        return jnp.einsum('kgrs,skd->rkgd', prob_low, value_rows, precision=HIGHEST)
    shaped = query_rows.reshape((block_count, TOK_DEV) + query_rows.shape[1:])
    result = lax.map(jax.checkpoint(per_block), (shaped, position.reshape(block_count, TOK_DEV), segment.reshape(block_count, TOK_DEV)))
    return result.reshape(query_rows.shape)

def forward(token_vals, extra_vals, params, position, segment, relative):
    q_mat, k_mat, v_mat, o_mat, left_mat, right_mat, gain_rows, qk_rows, gate_mat, up_mat, down_mat, pgate_mat, pproj_mat = [low(weight_in) for weight_in in params]
    seq_len = token_vals.shape[0]
    normed = rms_norm(token_vals, gain_rows[0])
    normed_low = low(normed)
    cos_tab, sine_tab = tables(relative, HD)
    q_raw = low_back(matmul_hi(normed_low, q_mat)).reshape(seq_len, H, HD)
    k_raw = low_back(matmul_hi(normed_low, k_mat)).reshape(seq_len, KVH, HD)
    v_raw = low_back(matmul_hi(normed_low, v_mat)).reshape(seq_len, KVH, HD)
    query_rows = low(rotate(rms_norm(q_raw, qk_rows[0]), cos_tab, sine_tab))
    key_rows = low(rotate(rms_norm(k_raw, qk_rows[1]), cos_tab, sine_tab))
    value_rows = low(rms_norm(v_raw, 1.0))
    head_out = attend(query_rows.reshape(seq_len, KVH, H // KVH, HD), key_rows, value_rows, position, segment)
    heads_low = low(low_back(head_out.reshape(seq_len, H * HD)))
    projected = low_back(matmul_hi(heads_low, o_mat))
    gated_sum = token_vals + rms_norm(projected, gain_rows[1])
    left_low = low(low_back(matmul_hi(normed_low, left_mat)))
    right_out = low_back(matmul_hi(left_low, right_mat))
    laurel = normed + rms_norm(right_out, gain_rows[2])
    joined = (gated_sum + laurel) * HALF_ROOT
    ff_in = low(rms_norm(joined, gain_rows[3]))
    gate_proj = low_back(matmul_hi(ff_in, gate_mat))
    up_proj = low_back(matmul_hi(ff_in, up_mat))
    hidden = low(gelu_tanh(gate_proj) * up_proj)
    down_proj = low_back(matmul_hi(hidden, down_mat))
    after_ff = joined + rms_norm(down_proj, gain_rows[4])
    per_gate = low_back(matmul_hi(low(after_ff), pgate_mat))
    per_mix = low(gelu_tanh(per_gate) * extra_vals)
    per_out = low_back(matmul_hi(per_mix, pproj_mat))
    return after_ff + rms_norm(per_out, gain_rows[5])

def reference(tokens, layer_input, cotangent, doc_lengths, pair_of, w_query, w_key, w_value, w_out, w_left, w_right, norm_gains, qk_gain, w_gate, w_up, w_down, w_pgate, w_pproj):

    def layouts_of(lengths):
        return layout(pair_of, lengths, TOK_DEV)
    position, segment, relative = jax.vmap(layouts_of)(doc_lengths)
    params = (w_query, w_key, w_value, w_out, w_left, w_right, norm_gains, qk_gain, w_gate, w_up, w_down, w_pgate, w_pproj)

    def whole_layer(token_vals, extra_vals, weights_in):

        def per_stream(stream_args):
            return forward(stream_args[0], stream_args[1], weights_in, stream_args[2], stream_args[3], stream_args[4])
        return lax.map(per_stream, (token_vals, extra_vals, position, segment, relative))
    outputs, pullback = jax.vjp(whole_layer, tokens.astype(jnp.float32), layer_input.astype(jnp.float32), params)
    d_tokens, d_extra, d_params = pullback(cotangent.astype(jnp.float32))
    return (outputs.astype(jnp.bfloat16), d_tokens.astype(jnp.bfloat16), d_extra.astype(jnp.bfloat16), d_params[0], d_params[1], d_params[2], d_params[3], d_params[4], d_params[5], d_params[6], d_params[7], d_params[8], d_params[9], d_params[10], d_params[11], d_params[12])
```

```python
import jax
import jax.numpy as jnp
from jax import lax
from jax.experimental import pallas as pl
from jax.experimental.pallas import tpu as pltpu
from jax.sharding import Mesh, PartitionSpec as P

H = 8
KVH = 2
HD = 256
Z = 4
X = 2
C = 2

EPSILON = 1e-06
ROPE_BASE = 1000000.0
HALF_ROOT = 0.7071067811865476
MASKED = -1e30
BF = jnp.bfloat16
F32 = jnp.float32
EVERY = ("z", "y", "x", "c")


def rms_norm(values_in, gain_in):
    return (
        values_in
        * lax.rsqrt(jnp.mean(values_in * values_in, axis=-1, keepdims=True) + EPSILON)
        * gain_in
    )


def unit_norm(values_in):
    return values_in * lax.rsqrt(
        jnp.mean(values_in * values_in, axis=-1, keepdims=True) + EPSILON
    )


def gelu_tanh(values_in):
    return jax.nn.gelu(values_in, approximate=True)


def glu_piece(gate_in, up_in):
    return gelu_tanh(gate_in) * up_in


def rotate(values_in, cos_tab, sine_tab):
    half_width = values_in.shape[-1] // 2
    first_half = values_in[..., :half_width]
    second_half = values_in[..., half_width:]
    return jnp.concatenate(
        [
            first_half * cos_tab - second_half * sine_tab,
            second_half * cos_tab + first_half * sine_tab,
        ],
        axis=-1,
    )


def times(left_in, right_in):
    return jnp.einsum("...a,ab->...b", left_in, right_in, preferred_element_type=F32)


def times_t(left_in, right_in):
    return jnp.einsum("...a,ba->...b", left_in, right_in, preferred_element_type=F32)


def over_rows(left_in, right_in):
    return jnp.einsum("ra,rb->ab", left_in, right_in, preferred_element_type=F32)


def give_to(value, axis, size, step):
    return lax.ppermute(value, axis, [(i, (i + step) % size) for i in range(size)])


def swap_core(value):
    return lax.ppermute(value, "c", [(0, 1), (1, 0)])


def after(value, *others):
    return lax.optimization_barrier((value, *others))[0]


def pick(value, index, axis):
    return lax.dynamic_index_in_dim(value, index, axis, keepdims=False)


def stage(*values):
    return lax.optimization_barrier(values)


def start_of(spec):
    return spec[0] * spec[1] if isinstance(spec, tuple) else spec


def shuffle(arrays, outs, copies):
    dtype = arrays[0].dtype
    aligned = True
    for _, r_in, c_in, _, r_out, c_out, height, wide in copies:
        for spec, tile in ((r_in, 16), (r_out, 16), (c_in, 128), (c_out, 128)):
            size = spec[1] if isinstance(spec, tuple) else spec
            aligned = aligned and size % tile == 0
        aligned = aligned and height % 16 == 0 and wide % 128 == 0
    if not aligned:
        made = [jnp.zeros(shape, dtype) for shape in outs]
        for a, r_in, c_in, o, r_out, c_out, height, wide in copies:
            piece = lax.dynamic_slice(
                arrays[a], (start_of(r_in), start_of(c_in)), (height, wide)
            )
            made[o] = lax.dynamic_update_slice(made[o], piece, (start_of(r_out), start_of(c_out)))
        return made
    numbers = []

    def known(spec):
        if not isinstance(spec, tuple):
            return spec
        numbers.append(spec[0])
        return (len(numbers) - 1, spec[1])

    plan = [
        (a, known(r_in), known(c_in), o, known(r_out), known(c_out), height, wide)
        for a, r_in, c_in, o, r_out, c_out, height, wide in copies
    ]
    table = jnp.stack([jnp.asarray(n, jnp.int32) for n in numbers] or [jnp.int32(0)])
    count = len(arrays)

    def kernel(table_ref, *refs):
        ins, made = refs[:count], refs[count:]

        def at(spec):
            if isinstance(spec, tuple):
                return pl.multiple_of(table_ref[spec[0]] * spec[1], spec[1])
            return spec

        for a, r_in, c_in, o, r_out, c_out, height, wide in plan:
            from_row, from_column, to_row, to_column = at(r_in), at(c_in), at(r_out), at(c_out)
            step = 16 if height % 32 else 32

            @pl.loop(0, height // step)
            def _(i):
                low = pl.multiple_of(i * step, step)
                made[o][pl.ds(to_row + low, step), pl.ds(to_column, wide)] = ins[a][
                    pl.ds(from_row + low, step), pl.ds(from_column, wide)
                ]

    moved = sum(height * wide for *_, height, wide in plan) * dtype.itemsize
    return pl.pallas_call(
        kernel,
        out_shape=[jax.ShapeDtypeStruct(shape, dtype) for shape in outs],
        grid_spec=pltpu.PrefetchScalarGridSpec(
            num_scalar_prefetch=1,
            grid=(1,),
            in_specs=[pl.BlockSpec(memory_space=pltpu.VMEM)] * count,
            out_specs=[pl.BlockSpec(memory_space=pltpu.VMEM)] * len(outs),
        ),
        cost_estimate=pl.CostEstimate(flops=0, bytes_accessed=2 * moved, transcendentals=0),
    )(table, *arrays)


def stack_rows(pieces):
    if len(pieces) == 1:
        return pieces[0]
    copies = []
    low = 0
    for i, piece in enumerate(pieces):
        copies.append((i, 0, 0, 0, low, 0, *piece.shape))
        low += piece.shape[0]
    return shuffle(pieces, [(low, pieces[0].shape[1])], copies)[0]


def z_take(block):
    return [block if k == 0 else give_to(block, "z", Z, -k) for k in range(Z)]


def flat_step(step_y, step_x, y_count):
    return [
        (y * X + x, ((y + step_y) % y_count) * X + (x + step_x) % X)
        for y in range(y_count)
        for x in range(X)
    ]


def all_steps(y_count):
    return [(p // X, p % X) for p in range(1, y_count * X)]


def gather_first(block, y_count):
    if y_count == 2:
        return [give_to(block, "x", X, 1), give_to(block, "y", 2, 1)]
    return [
        lax.ppermute(block, ("y", "x"), flat_step(-dy, -dx, y_count)) for dy, dx in all_steps(y_count)
    ]


def gather_second(block, got, y_count):
    if y_count == 2:
        half = block.shape[0] // 2
        return got + [give_to(got[0][:half], "y", 2, 1), give_to(got[1][half:], "x", X, 1)]
    return got


def gather_parts(block, got, y_count):
    arrays = [block] + list(got)
    rows = block.shape[0]
    parts = [[(i, 0, rows)] for i in range(len(arrays))]
    if y_count == 2:
        parts = parts[:3] + [[(3, 0, rows // 2), (4, 0, rows // 2)]]
    return arrays, parts


def sum_first(pieces, y_count):
    if y_count == 2:
        half = pieces[3].shape[0] // 2
        return [give_to(pieces[3][:half], "x", X, 1), give_to(pieces[3][half:], "y", 2, 1)]
    return [
        lax.ppermute(pieces[dy * X + dx], ("y", "x"), flat_step(dy, dx, y_count))
        for dy, dx in all_steps(y_count)
    ]


def add_low(first_in, second_in):
    return (first_in.astype(F32) + second_in.astype(F32)).astype(BF)


def sum_second(pieces, got, y_count):
    if y_count == 2:
        half = pieces[3].shape[0] // 2
        to_y = jnp.concatenate([add_low(pieces[2][:half], got[0]), pieces[2][half:]], axis=0)
        to_x = jnp.concatenate([pieces[1][:half], add_low(pieces[1][half:], got[1])], axis=0)
        return [give_to(to_y, "y", 2, 1), give_to(to_x, "x", X, 1)]
    return got


def sum_total(pieces, got):
    total = pieces[0].astype(F32)
    for piece in got:
        total = total + piece.astype(F32)
    return total


def reduce_start(own, other):
    return own + swap_core(other.astype(BF)).astype(F32)


def reduce_end(total):
    rows = total.shape[0] // Z
    out = total[:rows]
    for k in (2, 1, 3):
        piece = total[k * rows : (k + 1) * rows].astype(BF)
        out = out + give_to(piece, "z", Z, k).astype(F32)
    return out


def write_rows(pieces, starts):
    rows, width = pieces[0].shape
    whole = jnp.zeros((rows * len(pieces), width), pieces[0].dtype)
    for piece, start in zip(pieces, starts):
        whole = lax.dynamic_update_slice_in_dim(whole, piece, start, 0)
    return whole


def z_send(sends):
    return [sends(k) if k == 0 else give_to(sends(k), "z", Z, k) for k in range(Z)]


def z_place(arrived, zi):
    rows, width = arrived[0].shape
    copies = [(k, 0, 0, 0, ((zi - k) % Z, rows), 0, rows, width) for k in range(Z)]
    return shuffle(arrived, [(Z * rows, width)], copies)[0]


def order_cores(own, other, first, axis):
    return jnp.concatenate(
        [jnp.where(first, own, other), jnp.where(first, other, own)], axis=axis
    )


def places(pair_of, lengths, ctx_ids, row_count):
    blocks_last = 2 * pair_of.shape[0] - 1
    half_rows = row_count // 2
    pair = pair_of[ctx_ids][:, None]
    row = jnp.arange(row_count, dtype=jnp.int32)[None, :]
    block = jnp.where(row < half_rows, pair, blocks_last - pair)
    position = (block * half_rows + row % half_rows).reshape(-1)
    ends = jnp.cumsum(lengths, dtype=jnp.int32)
    before = ends[None, :] <= position[:, None]
    segment = jnp.sum(before.astype(jnp.int32), axis=1, dtype=jnp.int32)
    start = jnp.sum(jnp.where(before, lengths[None, :], 0), axis=1, dtype=jnp.int32)
    return position, segment, position - start


def local(
    tokens,
    layer_input,
    cotangent,
    doc_lengths,
    pair_of,
    w_query,
    w_key,
    w_value,
    w_out,
    w_left,
    w_right,
    norm_gains,
    qk_gain,
    w_gate,
    w_up,
    w_down,
    w_pgate,
    w_pproj,
):
    rows = tokens.shape[1]
    width = tokens.shape[2]
    y_count = lax.axis_size("y")
    zi, yi, xi, ci = (lax.axis_index(name) for name in EVERY)
    first = ci == 0
    shard = w_query.shape[0]
    ff_shard = w_down.shape[0]
    yx = y_count * X
    unit = C * shard
    places_yx = [((yi + p // X) % y_count) * X + (xi + p % X) % X for p in range(yx)]
    tall = Z * unit

    def place_parts(block, got, cuts):
        arrays, parts = gather_parts(block, got, y_count)
        copies = []
        for p in range(yx):
            z = 0
            for i, _, height in parts[p]:
                for low in range(0, height, unit):
                    to = (z * yx + places_yx[p], unit)
                    for o, (left_edge, right_edge) in enumerate(cuts):
                        copies.append(
                            (i, low, left_edge, o, to, 0, unit, right_edge - left_edge)
                        )
                    z += 1
        outs = [(Z * yx * unit, high - low) for low, high in cuts]
        return shuffle(arrays, outs, copies)

    def place_blocks(block, got, height):
        arrays, parts = gather_parts(block, got, y_count)
        copies = []
        for p in range(yx):
            low = 0
            for i, _, part in parts[p]:
                to = (places_yx[p] * (height // part) + low // part, part)
                copies.append((i, 0, 0, 0, to, 0, part, block.shape[1]))
                low += part
        return shuffle(arrays, [(yx * height, block.shape[1])], copies)[0]

    def row_pieces(value):
        value = value.reshape(Z, yx, unit, -1)
        return [pick(value, places_yx[p], 1).reshape(tall, -1) for p in range(yx)]

    def column_pieces(halves):
        copies = []
        for p in range(yx):
            for h in range(C):
                for z in range(Z):
                    column = (z * yx + places_yx[p], unit)
                    copies.append(
                        (h, 0, column, p * C + h, 0, z * unit, halves[h].shape[0], unit)
                    )
        made = shuffle(list(halves), [(halves[0].shape[0], tall)] * (C * yx), copies)
        return [made[p * C : p * C + C] for p in range(yx)]

    def pair_cores(own, height):
        other = swap_core(own)
        last = own.shape[1]
        cores = [jnp.where(first, own, other), jnp.where(first, other, own)]
        return jnp.concatenate([core.reshape(-1, 1, height, last) for core in cores], axis=1)

    left_rank = w_left.shape[1]
    ple = w_pgate.shape[1]
    gain_count = norm_gains.shape[0]
    qk_shard = qk_gain.shape[1]
    ff_own = yx * ff_shard
    lanes = 2 * left_rank
    span = 3 * HD

    group_rows = Z * rows

    def z_block(value, k, height, axis=0):
        return lax.dynamic_slice_in_dim(value, (zi + k) % Z * height, height, axis=axis)

    qkv_low = jnp.concatenate([w_query, w_key, w_value], axis=1).astype(BF)
    qkv_got = swap_core(qkv_low)
    gain_pack = jnp.concatenate(
        [
            jnp.pad(norm_gains, ((0, 0), (0, lanes - shard))),
            jnp.pad(qk_gain, ((0, 0), (0, lanes - qk_shard))),
            jnp.zeros((shard - gain_count - 2, lanes), F32),
        ],
        axis=0,
    )
    misc = jnp.concatenate(
        [
            jnp.concatenate([w_left, w_right.T, w_pgate], axis=1),
            jnp.concatenate([gain_pack, w_pproj.T], axis=1),
        ],
        axis=0,
    ).astype(BF)

    copies = []
    for k in range(Z):
        z_to = (zi + k) % Z
        head = z_to * KVH // Z
        columns = [z_to * C + ci, H + head, H + KVH + head]
        for a, c_from in ((0, ci), (1, 1 - ci)):
            for j, column in enumerate(columns):
                copies.append((a, 0, (column, HD), k, (c_from, shard), j * HD, shard, HD))
        copies.append((2, 0, 0, k, 0, span, unit, misc.shape[1]))
    first_sends = shuffle(
        [qkv_low, qkv_got, misc], [(unit, span + misc.shape[1])] * Z, copies
    )
    first_arrived = z_send(lambda k: first_sends[k])
    gate_late, up_late, _ = stage(w_gate, w_up, qkv_got)
    ff_low = [gate_late.astype(BF), up_late.astype(BF)]
    ff_got = [swap_core(mat) for mat in ff_low]
    own_tokens, pair_of, first_arrived, ff_low, ff_got = stage(
        tokens[0], pair_of, first_arrived, ff_low, ff_got
    )

    token_take = z_take(own_tokens)
    first_rows = z_place(first_arrived, zi)
    first_got = gather_second(first_rows, gather_first(first_rows, y_count), y_count)
    copies = []
    for m in range(2):
        for k in range(Z):
            for a in range(yx):
                column = (((zi + k) % Z * yx + a) * C + ci, ff_shard)
                to = (m * Z + k, a * ff_shard)
                for source, c_from in ((m, ci), (2 + m, 1 - ci)):
                    copies.append(
                        (source, 0, column, to[0], (c_from, shard), to[1], shard, ff_shard)
                    )
    ff_sends = shuffle(list(ff_low) + list(ff_got), [(unit, ff_own)] * (2 * Z), copies)
    ff_sends = [ff_sends[:Z], ff_sends[Z:]]

    lengths = [doc_lengths[0], swap_core(doc_lengths)[0]]
    z_ids = (zi + jnp.arange(Z)) % Z
    own_ids = z_ids * y_count + yi
    key_ids = (z_ids[None, :] * y_count + ((yi + jnp.arange(y_count)) % y_count)[:, None]).reshape(-1)
    visible = []
    relative = []
    for lens in lengths:
        q_pos, q_seg, q_rel = places(pair_of, lens, own_ids, rows)
        k_pos, k_seg, _ = places(pair_of, lens, key_ids, rows)
        seen = (k_seg[None, :] == q_seg[:, None]) & (k_pos[None, :] <= q_pos[:, None])
        visible.append(seen.astype(F32))
        relative.append(q_rel)
    visible = jnp.stack(visible)
    relative = jnp.concatenate(relative)
    frequency = ROPE_BASE ** (-2.0 * jnp.arange(HD // 2, dtype=F32) / HD)
    angles = relative.astype(F32)[:, None] * frequency[None, :]
    cos_tab, sine_tab = jnp.cos(angles), jnp.sin(angles)
    token_take, first_rows, first_got, ff_sends, visible, cos_tab, sine_tab, w_out = stage(
        token_take, first_rows, first_got, ff_sends, visible, cos_tab, sine_tab, w_out
    )
    visible = visible > 0.5

    def rotated(raw_in, gain_in):
        return rotate(rms_norm(raw_in, gain_in), cos_tab, sine_tab)

    def rotated_own(raw_in, gain_in):
        return rotate(rms_norm(raw_in, gain_in), cos_tab[:group_rows], sine_tab[:group_rows])

    token_own = stack_rows(token_take)
    token_other = swap_core(token_own)
    gate_arrived = z_send(lambda k: ff_sends[0][k])
    qkv_mat, misc_all, small_late = place_parts(
        first_rows,
        first_got,
        [(0, span), (span, span + lanes), (span + lanes, span + lanes + ple)],
    )
    misc_all = pair_cores(misc_all, unit)
    gain_all = misc_all[:, :, shard : shard + gain_count + 2, :shard]
    gain_all = gain_all.reshape(-1, gain_count + 2, shard).transpose(1, 0, 2)
    gains = gain_all[:gain_count].reshape(gain_count, -1).astype(F32)
    qk = gain_all[gain_count:, :, :qk_shard].reshape(2, -1).astype(F32)
    unit_own = unit_norm(token_own.astype(F32))
    unit_other = unit_norm(token_other.astype(F32))
    normed_own = (unit_own * gains[0]).astype(BF)
    normed_other = (unit_other * gains[0]).astype(BF)
    qkv = jnp.concatenate([times(normed_own, qkv_mat), times(normed_other, qkv_mat)], axis=0)
    q_raw, k_raw, v_raw = qkv[:, :HD], qkv[:, HD : 2 * HD], qkv[:, 2 * HD :]
    query = rotated(q_raw, qk[0]).astype(BF).reshape(C, group_rows, HD)
    key = rotated(k_raw, qk[1]).astype(BF)
    value = unit_norm(v_raw).astype(BF)
    kv = jnp.concatenate([key, value], axis=-1).reshape(C, group_rows, 2 * HD)
    out_low = w_out.astype(BF)
    out_got = gather_first(out_low, y_count)
    kv, query, gate_arrived, out_low, out_got, misc_all, small_late = stage(
        kv,
        query,
        gate_arrived,
        out_low,
        out_got,
        misc_all,
        small_late,
    )

    up_arrived = z_send(lambda k: ff_sends[1][k])
    kv_own, kv_other = [kv[0]], [kv[1]]
    for k in range(1, y_count):
        piece = give_to(kv[0], "y", y_count, -k)
        kv_own.append(piece)
        kv_other.append(swap_core(piece))
    kv_all = jnp.stack([jnp.concatenate(kv_own), jnp.concatenate(kv_other)])
    key_all, value_all = kv_all[..., :HD], kv_all[..., HD:]
    out_rows = place_blocks(out_low, gather_second(out_low, out_got, y_count), shard)
    out_half = yx // 2 * shard
    out_got = swap_core(lax.dynamic_slice_in_dim(out_rows, (1 - ci) * out_half, out_half))
    copies = []
    for a in range(yx // 2):
        copies.append((0, (ci * (yx // 2) + a, shard), 0, 0, (a * C + ci, shard), 0, shard, width))
        copies.append((1, a * shard, 0, 0, (a * C + 1 - ci, shard), 0, shard, width))
    out_mat = shuffle([out_rows, out_got], [(HD, width)], copies)[0]
    scores = jnp.einsum("sqd,skd->sqk", query, key_all, preferred_element_type=F32)
    scores = jnp.where(visible, scores, MASKED)
    top = jnp.max(scores, axis=-1, keepdims=True)
    log_total = top + jnp.log(jnp.sum(jnp.exp(scores - top), axis=-1, keepdims=True))
    probs = jnp.exp(scores - log_total)
    probs_low = probs.astype(BF)
    head_out = jnp.einsum("sqk,skd->sqd", probs_low, value_all, preferred_element_type=F32)
    heads_low = head_out.astype(BF).reshape(C * group_rows, HD)
    heads_share = times(heads_low[group_rows:], out_mat)
    projected = reduce_start(times(heads_low[:group_rows], out_mat), heads_share)
    copies = [
        (m * Z + k, 0, 0, 0, ((zi - k) % Z, unit), m * ff_own, unit, ff_own)
        for m in range(2)
        for k in range(Z)
    ]
    gu_rows = shuffle(list(gate_arrived) + up_arrived, [(tall, 2 * ff_own)], copies)[0]
    projected, gu_rows, heads_low, misc_all, own_tokens, small_late = stage(
        projected, gu_rows, heads_low, misc_all, own_tokens, small_late
    )

    projected = reduce_end(projected)
    gu_got = gather_first(gu_rows, y_count)
    lr_mat = misc_all[:, :, :shard].reshape(-1, lanes)
    left_mat, right_mat = lr_mat[:, :left_rank], lr_mat[:, left_rank:]
    token_vals = own_tokens.astype(F32)
    normed = rms_norm(token_vals, gains[0])
    normed_low = normed.astype(BF)
    left_low = times(normed_low, left_mat).astype(BF)
    right_out = times_t(left_low, right_mat)
    laurel = normed + rms_norm(right_out, gains[2])
    projected, gu_rows, gu_got, laurel, down_late = stage(
        projected, gu_rows, gu_got, laurel, w_down
    )

    gated_sum = token_vals + rms_norm(projected, gains[1])
    joined = (gated_sum + laurel) * HALF_ROOT
    ff_in = rms_norm(joined, gains[3]).astype(BF)
    ff_take = z_take(ff_in)
    gu_got = gather_second(gu_rows, gu_got, y_count)
    down_low = after(down_late, gu_got[-1]).astype(BF)
    down_got = gather_first(down_low, y_count)
    ff_take, gu_rows, gu_got, down_low, down_got = stage(
        ff_take, gu_rows, gu_got, down_low, down_got
    )

    ff_rows = stack_rows(ff_take)
    ff_halves = [ff_rows, swap_core(ff_rows)]
    gu_mat = place_parts(gu_rows, gu_got, [(0, 2 * ff_own)])[0]
    down_got = gather_second(down_low, down_got, y_count)
    gate_proj, up_proj, hidden = [], [], []
    for half in ff_halves:
        gate_up = times(half, gu_mat)
        gate_proj.append(gate_up[:, :ff_own])
        up_proj.append(gate_up[:, ff_own:])
        hidden.append(glu_piece(gate_proj[-1], up_proj[-1]).astype(BF))
    down_mat = place_blocks(down_low, down_got, ff_shard)
    down_share = times(hidden[1], down_mat)
    down_proj = reduce_start(times(hidden[0], down_mat), down_share)
    down_proj, small_late = stage(down_proj, small_late)

    down_proj = reduce_end(down_proj)
    ple_rows = small_late.reshape(-1, C, shard, ple)
    ple_rows = jnp.concatenate([ple_rows[:, 0], ple_rows[:, 1]], axis=-1).reshape(-1, 2 * ple)
    ple_mat = pair_cores(ple_rows, shard).reshape(-1, 2 * ple)
    down_proj, ple_mat = stage(down_proj, ple_mat)
    pgate_mat, pproj_mat = ple_mat[:, :ple], ple_mat[:, ple:]

    extra_vals = layer_input[0].astype(F32)
    after_ff = joined + rms_norm(down_proj, gains[4])
    after_low = after_ff.astype(BF)
    per_gate = times(after_low, pgate_mat)
    per_mix = glu_piece(per_gate, extra_vals).astype(BF)
    per_out = times_t(per_mix, pproj_mat)
    d_output = cotangent[0].astype(F32)
    _, norm_pull = jax.vjp(rms_norm, per_out, gains[5])
    d_per_out, d_gain_ple = norm_pull(d_output)
    d_per_low = d_per_out.astype(BF)
    d_per_mix = times(d_per_low, pproj_mat)
    _, glu_pull = jax.vjp(glu_piece, per_gate, extra_vals)
    d_per_gate, d_extra = glu_pull(d_per_mix)
    d_pgate_low = d_per_gate.astype(BF)
    d_after = d_output + times_t(d_pgate_low, pgate_mat)
    _, norm_pull = jax.vjp(rms_norm, down_proj, gains[4])
    d_down, d_gain_post_ff = norm_pull(d_after)
    d_down_low = d_down.astype(BF)
    (
        d_down_low, after_late, d_pgate_late, d_per_late, per_mix_late, after_ff, per_out, d_gain_ple,
        d_gain_post_ff, d_extra,
    ) = stage(
        d_down_low, after_low, d_pgate_low, d_per_low, per_mix, after_ff, per_out, d_gain_ple,
        d_gain_post_ff, d_extra,
    )

    d_down_take = z_take(d_down_low)
    output = after_ff + rms_norm(per_out, gains[5])
    ple_grads = row_pieces(
        jnp.concatenate(
            [over_rows(after_late, d_pgate_late), over_rows(d_per_late, per_mix_late)], axis=1
        ).astype(BF)
    )
    ple_got = sum_second(ple_grads, sum_first(ple_grads, y_count), y_count)
    ple_sum = sum_total(ple_grads, ple_got).astype(BF)
    d_down_take, ple_sum = stage(d_down_take, ple_sum)

    d_down_rows = stack_rows(d_down_take)
    d_down_halves = [d_down_rows, swap_core(d_down_rows)]
    ple_arrived = z_send(lambda k: z_block(ple_sum, k, unit))
    d_gu_low = []
    for half in range(C):
        d_hidden = times_t(d_down_halves[half], down_mat)
        _, glu_pull = jax.vjp(glu_piece, gate_proj[half], up_proj[half])
        d_gate, d_up = glu_pull(d_hidden)
        d_gu_low.append(jnp.concatenate([d_gate.astype(BF), d_up.astype(BF)], axis=-1))
    term_share = times_t(d_gu_low[1], gu_mat)
    term = reduce_start(times_t(d_gu_low[0], gu_mat), term_share)
    term, d_gu_low, ple_arrived, ff_halves, hidden, d_down_halves = stage(
        term, d_gu_low, ple_arrived, ff_halves, hidden, d_down_halves
    )

    term = reduce_end(term)

    def own_core(total):
        keep = jnp.where(first, total[:shard], total[shard:])
        send = jnp.where(first, total[shard:], total[:shard])
        return keep + swap_core(send.astype(BF)).astype(F32)

    def both_rows(lefts, rights):
        return (over_rows(lefts[0], rights[0]) + over_rows(lefts[1], rights[1])).astype(BF)

    gu_grads = [None] * yx
    down_grads = [None] * yx
    ff_pieces = column_pieces(ff_halves)
    for p in reversed(range(yx)):
        gu_grads[p] = both_rows(ff_pieces[p], d_gu_low)
    gu_got = sum_first(gu_grads, y_count)
    for p in reversed(range(yx)):
        down_grads[p] = both_rows(
            [
                lax.dynamic_slice_in_dim(half, places_yx[p] * ff_shard, ff_shard, axis=1)
                for half in hidden
            ],
            d_down_halves,
        )
    if y_count == 2:
        down_grads[3] = after(down_grads[3], gu_got[0])
    down_got = sum_first(down_grads, y_count)
    term, gu_got, down_got, gu_grads, down_grads, ple_arrived = stage(
        term, gu_got, down_got, gu_grads, down_grads, ple_arrived
    )

    _, norm_pull = jax.vjp(rms_norm, joined, gains[3])
    d_joined_norm, d_gain_pre_ff = norm_pull(term)
    d_branch = (d_after + d_joined_norm) * HALF_ROOT
    _, norm_pull = jax.vjp(rms_norm, projected, gains[1])
    d_projected, d_gain_post_attn = norm_pull(d_branch)
    d_proj_low = d_projected.astype(BF)
    d_proj_low, d_branch, d_gain_pre_ff, d_gain_post_attn, right_out, normed_own, normed_other = stage(
        d_proj_low, d_branch, d_gain_pre_ff, d_gain_post_attn, right_out, normed_own, normed_other
    )

    d_proj_take = z_take(d_proj_low)
    gu_got = sum_second(gu_grads, gu_got, y_count)
    ple_total = own_core(sum(piece.astype(F32) for piece in ple_arrived))
    _, norm_pull = jax.vjp(rms_norm, right_out, gains[2])
    d_right, d_gain_laurel = norm_pull(d_branch)
    d_right_low = d_right.astype(BF)
    d_left_low = times(d_right_low, right_mat).astype(BF)
    d_normed_own = d_branch + times_t(d_left_low, left_mat)
    left_grads = jnp.concatenate(
        [over_rows(d_left_low, normed_low), over_rows(left_low, d_right_low)], axis=0
    ).astype(BF)
    normed_pieces = column_pieces((normed_own, normed_other))
    d_proj_take, gu_got, left_grads, normed_pieces, d_normed_own, ple_total = stage(
        d_proj_take, gu_got, left_grads, normed_pieces, d_normed_own, ple_total
    )

    def by_core(rows_in, blocks):
        even = jnp.concatenate(
            [rows_in[2 * j * shard : (2 * j + 1) * shard] for j in range(blocks)], axis=0
        )
        odd = jnp.concatenate(
            [rows_in[(2 * j + 1) * shard : (2 * j + 2) * shard] for j in range(blocks)], axis=0
        )
        return jnp.where(first, even, odd), swap_core(jnp.where(first, odd, even))

    d_proj_rows = stack_rows(d_proj_take)
    d_proj_halves = [d_proj_rows, swap_core(d_proj_rows)]
    gu_sum = sum_total(gu_grads, gu_got).astype(BF)
    gu_pair = by_core(gu_sum, Z)
    gu_cores = [jnp.where(first, *gu_pair), jnp.where(first, *gu_pair[::-1])]
    gu_arrived = [z_send(lambda k: z_block(gu_cores[0], k, shard))]
    down_got = sum_second(down_grads, down_got, y_count)
    d_heads = jnp.concatenate([times_t(half, out_mat) for half in d_proj_halves], axis=0)
    d_heads = d_heads.astype(BF).reshape(C, group_rows, HD)
    delta = jnp.sum(d_heads.astype(F32) * head_out, axis=-1, keepdims=True)
    d_probs = jnp.einsum("sqd,skd->sqk", d_heads, value_all, preferred_element_type=F32)
    d_scores = (probs * (d_probs - delta)).astype(BF)
    d_query = jnp.einsum("sqk,skd->sqd", d_scores, key_all, preferred_element_type=F32)
    d_key = jnp.einsum("sqk,sqd->skd", d_scores, query, preferred_element_type=F32)
    d_value = jnp.einsum("sqk,sqd->skd", probs_low, d_heads, preferred_element_type=F32)
    d_key = d_key.reshape(C, y_count, group_rows, HD)
    d_value = d_value.reshape(C, y_count, group_rows, HD)

    def kv_share(stream, k):
        return jnp.concatenate([d_key[stream, k], d_value[stream, k]], axis=-1)

    kv_give = [swap_core(kv_share(1, k).astype(BF)) for k in range(y_count)]
    kv_sum = [kv_share(0, k) + kv_give[k].astype(F32) for k in range(y_count)]
    kv_sum, d_query, gu_arrived, gu_last, d_proj_halves, heads_low, down_got = stage(
        kv_sum, d_query, gu_arrived, gu_cores[1], d_proj_halves, heads_low, down_got
    )

    gu_arrived = gu_arrived + [z_send(lambda k: z_block(gu_last, k, shard))]
    own_kv = kv_sum[0]
    for k in range(1, y_count):
        own_kv = own_kv + give_to(kv_sum[k].astype(BF), "y", y_count, k).astype(F32)
    _, rot_pull = jax.vjp(rotated, q_raw, qk[0])
    d_q_raw, d_gain_query = rot_pull(d_query.reshape(C * group_rows, HD))
    _, rot_pull = jax.vjp(rotated_own, k_raw[:group_rows], qk[1])
    d_k_raw, d_gain_key = rot_pull(own_kv[:, :HD])
    _, unit_pull = jax.vjp(unit_norm, v_raw[:group_rows])
    (d_v_raw,) = unit_pull(own_kv[:, HD:])
    d_q_low = d_q_raw.astype(BF)
    d_kv_low = jnp.concatenate([d_k_raw.astype(BF), d_v_raw.astype(BF)], axis=-1)
    d_own_low = jnp.concatenate([d_q_low[:group_rows], d_kv_low], axis=-1)
    part_other = times_t(d_q_low[group_rows:], qkv_mat[:, :HD])
    part_own = times_t(d_own_low, qkv_mat)
    d_normed = reduce_start(part_own, part_other)
    d_normed, part_own, part_other, d_q_low, d_kv_low, gu_arrived, down_grads, d_proj_halves = stage(
        d_normed, part_own, part_other, d_q_low, d_kv_low, gu_arrived, down_grads, d_proj_halves
    )

    d_normed = d_normed_own + reduce_end(d_normed)
    d_gain_input = (
        jnp.sum(part_own * unit_own, axis=0)
        + jnp.sum(part_other * unit_other, axis=0)
        + jnp.sum(d_normed_own * unit_norm(token_vals), axis=0)
    )
    d_qk = jnp.stack([d_gain_query, d_gain_key]).reshape(2, -1, qk_shard)
    d_qk = jnp.pad(d_qk, ((0, 0), (0, 0), (0, shard - qk_shard))).reshape(2, -1)
    gain_grads = jnp.stack(
        [d_gain_input, d_gain_post_attn, d_gain_laurel, d_gain_pre_ff, d_gain_post_ff, d_gain_ple]
    )
    gain_grads = jnp.concatenate([gain_grads, d_qk], axis=0)
    gain_grads = jnp.pad(gain_grads, ((0, 16 - gain_count - 2), (0, 0))).astype(BF)
    row_grads = jnp.concatenate([left_grads, gain_grads], axis=0)
    row_count = row_grads.shape[0]
    last_grads = []
    for p in range(yx):
        query_part = both_rows(normed_pieces[p], (d_q_low[:group_rows], d_q_low[group_rows:]))
        kv_part = over_rows(normed_pieces[p][0], d_kv_low).astype(BF)
        last_grads.append((query_part, kv_part))
    copies = []
    for p in range(yx):
        copies.append((C * p, 0, 0, p, 0, 0, tall, HD))
        copies.append((C * p + 1, 0, 0, p, 0, HD, tall, 2 * HD))
        for z in range(Z):
            column = (z * yx + places_yx[p], unit)
            copies.append((C * yx, 0, column, p, tall, z * unit, row_count, unit))
        copies.append((C * yx + 1, 0, 0, p, tall, tall, row_count, span - tall))
    last_grads = shuffle(
        [part for pair in last_grads for part in pair]
        + [row_grads, jnp.zeros((row_count, span - tall), BF)],
        [(tall + row_count, span)] * yx,
        copies,
    )
    last_got = sum_first(last_grads, y_count)
    last_got, last_grads, heads_low, d_proj_halves = stage(
        last_got, last_grads, heads_low, d_proj_halves
    )
    last_got = sum_second(last_grads, last_got, y_count)
    out_grad = both_rows((heads_low[:group_rows], heads_low[group_rows:]), d_proj_halves)
    out_both = order_cores(*by_core(out_grad, yx // 2), first, 0)
    out_grads = [
        lax.dynamic_slice_in_dim(out_both, places_yx[p] * shard, shard) for p in range(yx)
    ]
    grad_down = sum_total(down_grads, down_got)
    d_normed, last_got, last_grads, out_grads, gu_arrived = stage(
        d_normed, last_got, last_grads, out_grads, gu_arrived
    )

    last_low = sum_total(last_grads, last_got).astype(BF)
    qkv_pair = by_core(last_low[:tall], Z)
    qkv_cores = order_cores(*qkv_pair, first, 1)
    last_arrived = z_send(lambda k: z_block(qkv_cores, k, shard))
    by_row = last_low[tall:, :tall]
    row_arrived = z_send(lambda k: z_block(by_row, k, unit, axis=1))
    grad_out = sum_total(out_grads, sum_second(out_grads, sum_first(out_grads, y_count), y_count))
    _, norm_pull = jax.vjp(rms_norm, token_vals, gains[0])
    d_tokens_norm, _ = norm_pull(d_normed)
    d_tokens = d_branch + d_tokens_norm
    copies = []
    for k in range(Z):
        for c in range(C):
            for m in range(2):
                for a in range(yx):
                    column = (((zi - k) % Z * yx + a) * C + c, ff_shard)
                    copies.append(
                        (
                            c * Z + k, 0, m * ff_own + a * ff_shard,
                            m, 0, column, shard, ff_shard,
                        )
                    )
    grad_gu = shuffle(
        list(gu_arrived[0]) + list(gu_arrived[1]), [(shard, Z * yx * C * ff_shard)] * 2, copies
    )
    grad_gu = [grad.astype(F32) for grad in grad_gu]
    qkv_parts = z_place(last_arrived, zi).astype(F32)
    row_total = sum(piece.astype(F32) for piece in row_arrived)
    row_keep = jnp.where(first, row_total[:, :shard], row_total[:, shard:])
    row_send = jnp.where(first, row_total[:, shard:], row_total[:, :shard])
    row_total = row_keep + swap_core(row_send.astype(BF)).astype(F32)

    def qkv_part(z, c, m):
        return qkv_parts[z * shard : (z + 1) * shard, (3 * c + m) * HD : (3 * c + m + 1) * HD]

    grad_query = jnp.concatenate([qkv_part(z, c, 0) for z in range(Z) for c in range(C)], axis=1)
    grad_kv = [
        jnp.concatenate(
            [
                sum(
                    qkv_part(z, c, m)
                    for z in range(h * Z // KVH, (h + 1) * Z // KVH)
                    for c in range(C)
                )
                for h in range(KVH)
            ],
            axis=1,
        )
        for m in (1, 2)
    ]
    grad_gains = row_total[lanes : lanes + gain_count]
    grad_qk = row_total[lanes + gain_count : lanes + gain_count + 2, :qk_shard]
    return (
        output.astype(BF)[None],
        d_tokens.astype(BF)[None],
        d_extra.astype(BF)[None],
        grad_query,
        grad_kv[0],
        grad_kv[1],
        grad_out,
        row_total[:left_rank].T,
        row_total[left_rank:lanes],
        grad_gains,
        grad_qk,
        grad_gu[0],
        grad_gu[1],
        grad_down,
        ple_total[:, :ple],
        ple_total[:, ple:].T,
    )


def solution(mesh):
    fine = Mesh(mesh.devices.reshape(Z, -1, X, C), EVERY)
    rows = P(EVERY, None)
    cols = P(None, EVERY)
    stream = P(("x", "c"), ("z", "y"), None)
    return jax.shard_map(
        local,
        mesh=fine,
        in_specs=(
            stream, stream, stream, P(("x", "c"), None), P(),
            rows, rows, rows, rows, rows, cols, cols, cols, rows, rows, rows, rows, cols,
        ),
        out_specs=(
            stream, stream, stream,
            rows, rows, rows, rows, rows, cols, cols, cols, rows, rows, rows, rows, cols,
        ),
        check_vma=False,
    )
```

```python
import jax
import jax.numpy as jnp
from jax import lax
from jax.experimental import pallas as pl
from jax.experimental.pallas import tpu as pltpu
from jax.sharding import Mesh, PartitionSpec as P

H = 8
KVH = 2
HD = 256
Z = 4
X = 2
C = 2

EPSILON = 1e-06
ROPE_BASE = 1000000.0
HALF_ROOT = 0.7071067811865476
MASKED = -1e30
BF = jnp.bfloat16
F32 = jnp.float32
EVERY = ("z", "y", "x", "c")


def rms_norm(values_in, gain_in):
    return (
        values_in
        * lax.rsqrt(jnp.mean(values_in * values_in, axis=-1, keepdims=True) + EPSILON)
        * gain_in
    )


def unit_norm(values_in):
    return values_in * lax.rsqrt(
        jnp.mean(values_in * values_in, axis=-1, keepdims=True) + EPSILON
    )


def gelu_tanh(values_in):
    return jax.nn.gelu(values_in, approximate=True)


def glu_piece(gate_in, up_in):
    return gelu_tanh(gate_in) * up_in


def rotate(values_in, cos_tab, sine_tab):
    half_width = values_in.shape[-1] // 2
    first_half = values_in[..., :half_width]
    second_half = values_in[..., half_width:]
    return jnp.concatenate(
        [
            first_half * cos_tab - second_half * sine_tab,
            second_half * cos_tab + first_half * sine_tab,
        ],
        axis=-1,
    )


def times(left_in, right_in):
    return jnp.einsum("...a,ab->...b", left_in, right_in, preferred_element_type=F32)


def times_t(left_in, right_in):
    return jnp.einsum("...a,ba->...b", left_in, right_in, preferred_element_type=F32)


def over_rows(left_in, right_in):
    return jnp.einsum("ra,rb->ab", left_in, right_in, preferred_element_type=F32)


def give_to(value, axis, size, step):
    return lax.ppermute(value, axis, [(i, (i + step) % size) for i in range(size)])


def swap_core(value):
    return lax.ppermute(value, "c", [(0, 1), (1, 0)])


def after(value, *others):
    return lax.optimization_barrier((value, *others))[0]


def pick(value, index, axis):
    return lax.dynamic_index_in_dim(value, index, axis, keepdims=False)


def stage(*values):
    return lax.optimization_barrier(values)


def start_of(spec):
    return spec[0] * spec[1] if isinstance(spec, tuple) else spec


def shuffle(arrays, outs, copies):
    dtype = arrays[0].dtype
    aligned = True
    for _, r_in, c_in, _, r_out, c_out, height, wide in copies:
        for spec, tile in ((r_in, 16), (r_out, 16), (c_in, 128), (c_out, 128)):
            size = spec[1] if isinstance(spec, tuple) else spec
            aligned = aligned and size % tile == 0
        aligned = aligned and height % 16 == 0 and wide % 128 == 0
    if not aligned:
        made = [jnp.zeros(shape, dtype) for shape in outs]
        for a, r_in, c_in, o, r_out, c_out, height, wide in copies:
            piece = lax.dynamic_slice(
                arrays[a], (start_of(r_in), start_of(c_in)), (height, wide)
            )
            made[o] = lax.dynamic_update_slice(made[o], piece, (start_of(r_out), start_of(c_out)))
        return made
    numbers = []

    def known(spec):
        if not isinstance(spec, tuple):
            return spec
        numbers.append(spec[0])
        return (len(numbers) - 1, spec[1])

    plan = [
        (a, known(r_in), known(c_in), o, known(r_out), known(c_out), height, wide)
        for a, r_in, c_in, o, r_out, c_out, height, wide in copies
    ]
    table = jnp.stack([jnp.asarray(n, jnp.int32) for n in numbers] or [jnp.int32(0)])
    count = len(arrays)

    def kernel(table_ref, *refs):
        ins, made = refs[:count], refs[count:]

        def at(spec):
            if isinstance(spec, tuple):
                return pl.multiple_of(table_ref[spec[0]] * spec[1], spec[1])
            return spec

        for a, r_in, c_in, o, r_out, c_out, height, wide in plan:
            from_row, from_column, to_row, to_column = at(r_in), at(c_in), at(r_out), at(c_out)
            step = 16
            while height % (2 * step) == 0 and 2 * step * wide <= 65536:
                step *= 2
            chunks = height // step

            def move(low):
                made[o][pl.ds(to_row + low, step), pl.ds(to_column, wide)] = ins[a][
                    pl.ds(from_row + low, step), pl.ds(from_column, wide)
                ]

            if chunks % 4 or chunks <= 8:
                for i in range(chunks):
                    move(i * step)
            else:

                @pl.loop(0, chunks // 4)
                def _(i):
                    for j in range(4):
                        move(pl.multiple_of(i * 4 * step, step) + j * step)

    moved = sum(height * wide for *_, height, wide in plan) * dtype.itemsize
    return pl.pallas_call(
        kernel,
        out_shape=[jax.ShapeDtypeStruct(shape, dtype) for shape in outs],
        grid_spec=pltpu.PrefetchScalarGridSpec(
            num_scalar_prefetch=1,
            grid=(1,),
            in_specs=[pl.BlockSpec(memory_space=pltpu.VMEM)] * count,
            out_specs=[pl.BlockSpec(memory_space=pltpu.VMEM)] * len(outs),
        ),
        cost_estimate=pl.CostEstimate(flops=0, bytes_accessed=2 * moved, transcendentals=0),
    )(table, *arrays)


def stack_rows(pieces):
    if len(pieces) == 1:
        return pieces[0]
    copies = []
    low = 0
    for i, piece in enumerate(pieces):
        copies.append((i, 0, 0, 0, low, 0, *piece.shape))
        low += piece.shape[0]
    return shuffle(pieces, [(low, pieces[0].shape[1])], copies)[0]


def z_take(block):
    return [block if k == 0 else give_to(block, "z", Z, -k) for k in range(Z)]


def flat_step(step_y, step_x, y_count):
    return [
        (y * X + x, ((y + step_y) % y_count) * X + (x + step_x) % X)
        for y in range(y_count)
        for x in range(X)
    ]


def all_steps(y_count):
    return [(p // X, p % X) for p in range(1, y_count * X)]


def gather_first(block, y_count):
    if y_count == 2:
        return [give_to(block, "x", X, 1), give_to(block, "y", 2, 1)]
    return [
        lax.ppermute(block, ("y", "x"), flat_step(-dy, -dx, y_count)) for dy, dx in all_steps(y_count)
    ]


def gather_second(block, got, y_count):
    if y_count == 2:
        half = block.shape[0] // 2
        return got + [give_to(got[0][:half], "y", 2, 1), give_to(got[1][half:], "x", X, 1)]
    return got


def gather_parts(block, got, y_count):
    arrays = [block] + list(got)
    rows = block.shape[0]
    parts = [[(i, 0, rows)] for i in range(len(arrays))]
    if y_count == 2:
        parts = parts[:3] + [[(3, 0, rows // 2), (4, 0, rows // 2)]]
    return arrays, parts


def sum_first(pieces, y_count):
    if y_count == 2:
        half = pieces[3].shape[0] // 2
        return [give_to(pieces[3][:half], "x", X, 1), give_to(pieces[3][half:], "y", 2, 1)]
    return [
        lax.ppermute(pieces[dy * X + dx], ("y", "x"), flat_step(dy, dx, y_count))
        for dy, dx in all_steps(y_count)
    ]


def add_low(first_in, second_in):
    return (first_in.astype(F32) + second_in.astype(F32)).astype(BF)


def sum_second(pieces, got, y_count):
    if y_count == 2:
        half = pieces[3].shape[0] // 2
        to_y = jnp.concatenate([add_low(pieces[2][:half], got[0]), pieces[2][half:]], axis=0)
        to_x = jnp.concatenate([pieces[1][:half], add_low(pieces[1][half:], got[1])], axis=0)
        return [give_to(to_y, "y", 2, 1), give_to(to_x, "x", X, 1)]
    return got


def sum_total(pieces, got):
    return add_up([pieces[0]] + list(got))


def core_sum(own, other):
    total = own + swap_core(other.astype(BF)).astype(F32)
    rows = total.shape[0] // Z
    return [total[:rows]] + [
        total[k * rows : (k + 1) * rows].astype(BF) for k in range(1, Z)
    ]


def z_shares(blocks):
    return [blocks[0]] + [give_to(blocks[k], "z", Z, k) for k in range(1, Z)]


def add_up(pieces):
    total = pieces[0].astype(F32)
    for piece in pieces[1:]:
        total = total + piece.astype(F32)
    return total


def write_rows(pieces, starts):
    rows, width = pieces[0].shape
    whole = jnp.zeros((rows * len(pieces), width), pieces[0].dtype)
    for piece, start in zip(pieces, starts):
        whole = lax.dynamic_update_slice_in_dim(whole, piece, start, 0)
    return whole


def z_send(sends):
    return [sends(k) if k == 0 else give_to(sends(k), "z", Z, k) for k in range(Z)]


def z_place(arrived, zi):
    rows, width = arrived[0].shape
    copies = [(k, 0, 0, 0, ((zi - k) % Z, rows), 0, rows, width) for k in range(Z)]
    return shuffle(arrived, [(Z * rows, width)], copies)[0]


def order_cores(own, other, first, axis):
    return jnp.concatenate(
        [jnp.where(first, own, other), jnp.where(first, other, own)], axis=axis
    )


def places(pair_of, lengths, ctx_ids, row_count):
    blocks_last = 2 * pair_of.shape[0] - 1
    half_rows = row_count // 2
    pair = pair_of[ctx_ids][:, None]
    row = jnp.arange(row_count, dtype=jnp.int32)[None, :]
    block = jnp.where(row < half_rows, pair, blocks_last - pair)
    position = (block * half_rows + row % half_rows).reshape(-1)
    ends = jnp.cumsum(lengths, dtype=jnp.int32)
    before = ends[None, :] <= position[:, None]
    segment = jnp.sum(before.astype(jnp.int32), axis=1, dtype=jnp.int32)
    start = jnp.sum(jnp.where(before, lengths[None, :], 0), axis=1, dtype=jnp.int32)
    return position, segment, position - start


def local(
    tokens,
    layer_input,
    cotangent,
    doc_lengths,
    pair_of,
    w_query,
    w_key,
    w_value,
    w_out,
    w_left,
    w_right,
    norm_gains,
    qk_gain,
    w_gate,
    w_up,
    w_down,
    w_pgate,
    w_pproj,
):
    rows = tokens.shape[1]
    width = tokens.shape[2]
    y_count = lax.axis_size("y")
    zi, yi, xi, ci = (lax.axis_index(name) for name in EVERY)
    first = ci == 0
    shard = w_query.shape[0]
    ff_shard = w_down.shape[0]
    yx = y_count * X
    unit = C * shard
    places_yx = [((yi + p // X) % y_count) * X + (xi + p % X) % X for p in range(yx)]
    tall = Z * unit

    def place_parts(block, got, cuts):
        arrays, parts = gather_parts(block, got, y_count)
        copies = []
        for p in range(yx):
            z = 0
            for i, _, height in parts[p]:
                for low in range(0, height, unit):
                    to = (z * yx + places_yx[p], unit)
                    for o, (left_edge, right_edge) in enumerate(cuts):
                        copies.append(
                            (i, low, left_edge, o, to, 0, unit, right_edge - left_edge)
                        )
                    z += 1
        outs = [(Z * yx * unit, high - low) for low, high in cuts]
        return shuffle(arrays, outs, copies)

    def place_blocks(block, got, height):
        arrays, parts = gather_parts(block, got, y_count)
        copies = []
        for p in range(yx):
            low = 0
            for i, _, part in parts[p]:
                to = (places_yx[p] * (height // part) + low // part, part)
                copies.append((i, 0, 0, 0, to, 0, part, block.shape[1]))
                low += part
        return shuffle(arrays, [(yx * height, block.shape[1])], copies)[0]

    def row_pieces(value):
        value = value.reshape(Z, yx, unit, -1)
        return [pick(value, places_yx[p], 1).reshape(tall, -1) for p in range(yx)]

    def column_pieces(halves):
        copies = []
        for p in range(yx):
            for h in range(C):
                for z in range(Z):
                    column = (z * yx + places_yx[p], unit)
                    copies.append(
                        (h, 0, column, p * C + h, 0, z * unit, halves[h].shape[0], unit)
                    )
        made = shuffle(list(halves), [(halves[0].shape[0], tall)] * (C * yx), copies)
        return [made[p * C : p * C + C] for p in range(yx)]

    def pair_cores(own, height):
        other = swap_core(own)
        last = own.shape[1]
        cores = [jnp.where(first, own, other), jnp.where(first, other, own)]
        return jnp.concatenate([core.reshape(-1, 1, height, last) for core in cores], axis=1)

    left_rank = w_left.shape[1]
    ple = w_pgate.shape[1]
    gain_count = norm_gains.shape[0]
    qk_shard = qk_gain.shape[1]
    ff_own = yx * ff_shard
    lanes = 2 * left_rank
    span = 3 * HD

    group_rows = Z * rows

    def z_block(value, k, height, axis=0):
        return lax.dynamic_slice_in_dim(value, (zi + k) % Z * height, height, axis=axis)

    gain_pack = jnp.concatenate(
        [
            jnp.pad(norm_gains, ((0, 0), (0, lanes - shard))),
            jnp.pad(qk_gain, ((0, 0), (0, lanes - qk_shard))),
        ],
        axis=0,
    )
    gain_rows = gain_count + 2
    qkv_low = jnp.concatenate(
        [w_query, w_key, w_value, jnp.pad(gain_pack, ((0, shard - gain_rows), (0, 0)))], axis=1
    ).astype(BF)
    qkv_got = swap_core(qkv_low)
    qkv_low, qkv_got, out_late = stage(qkv_low, qkv_got, w_out)

    gain_low = (H + 2 * KVH) * HD
    own_gain, other_gain = qkv_low[:gain_rows, gain_low:], qkv_got[:gain_rows, gain_low:]
    gain_block = jnp.concatenate(
        [
            jnp.where(first, own_gain, other_gain),
            jnp.where(first, other_gain, own_gain),
            jnp.zeros((max(shard - C * gain_rows, 0), lanes), BF),
        ],
        axis=0,
    )[:shard]
    misc = jnp.concatenate(
        [
            jnp.concatenate([w_left, w_right.T, w_pgate], axis=1).astype(BF),
            jnp.concatenate([gain_block, w_pproj.T.astype(BF)], axis=1),
        ],
        axis=0,
    )
    copies = []
    for k in range(Z):
        z_to = (zi + k) % Z
        head = z_to * KVH // Z
        columns = [z_to * C + ci, H + head, H + KVH + head]
        for a, c_from in ((0, ci), (1, 1 - ci)):
            for j, column in enumerate(columns):
                copies.append((a, 0, (column, HD), k, (c_from, shard), j * HD, shard, HD))
        copies.append((2, 0, 0, k, 0, span, unit, misc.shape[1]))
    first_sends = shuffle(
        [qkv_low, qkv_got, misc], [(unit, span + misc.shape[1])] * Z, copies
    )
    first_arrived = z_send(lambda k: first_sends[k])
    gate_late, up_late, out_late, _ = stage(w_gate, w_up, out_late, first_sends)
    ff_low = jnp.concatenate([gate_late, up_late], axis=1).astype(BF)
    ff_got = swap_core(ff_low)
    out_low = out_late.astype(BF)
    out_x = give_to(out_low, "x", X, 1) if y_count == 2 else out_low
    own_tokens, pair_of, first_arrived, ff_low, ff_got, out_low, out_x = stage(
        tokens[0], pair_of, first_arrived, ff_low, ff_got, out_low, out_x
    )

    token_take = z_take(own_tokens)
    first_rows = z_place(first_arrived, zi)
    first_got = gather_first(first_rows, y_count)
    copies = []
    for m in range(2):
        for k in range(Z):
            for a in range(yx):
                column = (((m * Z + (zi + k) % Z) * yx + a) * C + ci, ff_shard)
                for source, c_from in ((0, ci), (1, 1 - ci)):
                    copies.append(
                        (
                            source, 0, column, m * Z + k, (c_from, shard), a * ff_shard,
                            shard, ff_shard,
                        )
                    )
    ff_sends = shuffle([ff_low, ff_got], [(unit, ff_own)] * (2 * Z), copies)
    ff_sends = [ff_sends[:Z], ff_sends[Z:]]
    out_pair = stack_rows([out_low, out_x])
    first_rows, first_got = stage(first_rows, first_got)
    first_got = gather_second(first_rows, list(first_got), y_count)

    lengths = [doc_lengths[0], swap_core(doc_lengths)[0]]
    z_ids = (zi + jnp.arange(Z)) % Z
    own_ids = z_ids * y_count + yi
    key_ids = (z_ids[None, :] * y_count + ((yi + jnp.arange(y_count)) % y_count)[:, None]).reshape(-1)
    visible = []
    relative = []
    for lens in lengths:
        q_pos, q_seg, q_rel = places(pair_of, lens, own_ids, rows)
        k_pos, k_seg, _ = places(pair_of, lens, key_ids, rows)
        seen = (k_seg[None, :] == q_seg[:, None]) & (k_pos[None, :] <= q_pos[:, None])
        visible.append(seen.astype(F32))
        relative.append(q_rel)
    visible = jnp.stack(visible)
    relative = jnp.concatenate(relative)
    frequency = ROPE_BASE ** (-2.0 * jnp.arange(HD // 2, dtype=F32) / HD)
    angles = relative.astype(F32)[:, None] * frequency[None, :]
    cos_tab, sine_tab = jnp.cos(angles), jnp.sin(angles)
    (
        token_take, first_rows, first_got, ff_sends, visible, cos_tab, sine_tab, out_pair
    ) = stage(
        token_take, first_rows, first_got, ff_sends, visible, cos_tab, sine_tab, out_pair
    )
    visible = visible > 0.5

    def rotated(raw_in, gain_in):
        return rotate(rms_norm(raw_in, gain_in), cos_tab, sine_tab)

    def rotated_own(raw_in, gain_in):
        return rotate(rms_norm(raw_in, gain_in), cos_tab[:group_rows], sine_tab[:group_rows])

    token_own = stack_rows(token_take)
    token_other = swap_core(token_own)
    gate_arrived = z_send(lambda k: ff_sends[0][k])
    qkv_mat, misc_all, small_late = place_parts(
        first_rows,
        first_got,
        [(0, span), (span, span + lanes), (span + lanes, span + lanes + ple)],
    )
    gain_all = misc_all.reshape(-1, unit, lanes)[:, shard : shard + C * gain_rows, :shard]
    gain_all = gain_all.reshape(-1, gain_rows, shard).transpose(1, 0, 2)
    gains = gain_all[:gain_count].reshape(gain_count, -1).astype(F32)
    qk = gain_all[gain_count:, :, :qk_shard].reshape(2, -1).astype(F32)
    lr_own = misc_all.reshape(-1, unit, lanes)[:, :shard].reshape(-1, lanes)
    unit_own = unit_norm(token_own.astype(F32))
    unit_other = unit_norm(token_other.astype(F32))
    normed_own = (unit_own * gains[0]).astype(BF)
    normed_other = (unit_other * gains[0]).astype(BF)
    qkv = jnp.concatenate([times(normed_own, qkv_mat), times(normed_other, qkv_mat)], axis=0)
    q_raw, k_raw, v_raw = qkv[:, :HD], qkv[:, HD : 2 * HD], qkv[:, 2 * HD :]
    query = rotated(q_raw, qk[0]).astype(BF).reshape(C, group_rows, HD)
    key = rotated(k_raw, qk[1]).astype(BF)
    value = unit_norm(v_raw).astype(BF)
    kv = jnp.concatenate([key, value], axis=-1).reshape(C, group_rows, 2 * HD)
    out_y = give_to(out_pair, "y", 2, 1) if y_count == 2 else out_pair
    kv, query, gate_arrived, out_pair, out_y, lr_own, small_own = stage(
        kv, query, gate_arrived, out_pair, out_y, lr_own, small_late
    )

    kv_own = [kv[0]] + [give_to(kv[0], "y", y_count, -k) for k in range(1, y_count)]
    lr_other = swap_core(lr_own)
    small_other = swap_core(small_own)
    if y_count == 2:
        copies = []
        for p in range(yx):
            copies.append(
                (p // X, p % X * shard, 0, 0, (places_yx[p], shard), 0, shard, width)
            )
        out_rows = shuffle([out_pair, out_y], [(yx * shard, width)], copies)[0]
        out_half = yx // 2 * shard
        out_got = swap_core(lax.dynamic_slice_in_dim(out_rows, (1 - ci) * out_half, out_half))
    else:
        out_rows = lax.all_gather(out_pair[:shard], ("y", "x", "c"), axis=0, tiled=True)
        out_got = out_rows
    kv_own, lr_other, small_other, out_rows, out_got = stage(
        kv_own, lr_other, small_other, out_rows, out_got
    )

    if y_count == 2:
        copies = []
        for a in range(yx // 2):
            copies.append(
                (0, (ci * (yx // 2) + a, shard), 0, 0, (a * C + ci, shard), 0, shard, width)
            )
            copies.append((1, a * shard, 0, 0, (a * C + 1 - ci, shard), 0, shard, width))
        out_mat = shuffle([out_rows, out_got], [(HD, width)], copies)[0]
    else:
        out_mat = lax.dynamic_slice_in_dim(out_rows, ci * HD, HD)
    up_arrived = z_send(lambda k: ff_sends[1][k])
    kv_other = [kv[1]] + [swap_core(piece) for piece in kv_own[1:]]
    kv_all = jnp.stack([jnp.concatenate(kv_own), jnp.concatenate(kv_other)])
    key_all, value_all = kv_all[..., :HD], kv_all[..., HD:]
    scores = jnp.einsum("sqd,skd->sqk", query, key_all, preferred_element_type=F32)
    scores = jnp.where(visible, scores, MASKED)
    top = jnp.max(scores, axis=-1, keepdims=True)
    log_total = top + jnp.log(jnp.sum(jnp.exp(scores - top), axis=-1, keepdims=True))
    probs = jnp.exp(scores - log_total)
    probs_low = probs.astype(BF)
    head_out = jnp.einsum("sqk,skd->sqd", probs_low, value_all, preferred_element_type=F32)
    heads_low = head_out.astype(BF).reshape(C * group_rows, HD)
    heads_low, up_arrived, out_mat = stage(heads_low, up_arrived, out_mat)

    copies = [
        (m * Z + k, 0, 0, 0, ((zi - k) % Z, unit), m * ff_own, unit, ff_own)
        for m in range(2)
        for k in range(Z)
    ]
    heads_share = times(heads_low[group_rows:], out_mat)
    gu_rows = shuffle(list(gate_arrived) + list(up_arrived), [(tall, 2 * ff_own)], copies)[0]
    blocks = core_sum(times(heads_low[:group_rows], out_mat), heads_share)
    blocks, gu_rows, lr_own, lr_other, own_tokens, heads_low = stage(
        blocks, gu_rows, lr_own, lr_other, own_tokens, heads_low
    )
    shares = z_shares(blocks)
    gu_got = gather_first(gu_rows, y_count)

    def core_rows(own, other):
        last = own.shape[1]
        cores = [jnp.where(first, own, other), jnp.where(first, other, own)]
        return jnp.concatenate(
            [core.reshape(-1, 1, shard, last) for core in cores], axis=1
        ).reshape(-1, last)

    lr_mat = core_rows(lr_own, lr_other)
    left_mat, right_mat = lr_mat[:, :left_rank], lr_mat[:, left_rank:]
    token_vals = own_tokens.astype(F32)
    normed = rms_norm(token_vals, gains[0])
    normed_low = normed.astype(BF)
    left_low = times(normed_low, left_mat).astype(BF)
    right_out = times_t(left_low, right_mat)
    laurel = normed + rms_norm(right_out, gains[2])
    shares, gu_rows, gu_got, laurel, w_down = stage(shares, gu_rows, gu_got, laurel, w_down)

    projected = add_up(shares)
    gated_sum = token_vals + rms_norm(projected, gains[1])
    joined = (gated_sum + laurel) * HALF_ROOT
    ff_in = rms_norm(joined, gains[3]).astype(BF)
    ff_in, gu_got, gu_rows, w_down = stage(ff_in, gu_got, gu_rows, w_down)
    ff_take = z_take(ff_in)
    down_low = w_down.astype(BF)
    if y_count == 2:
        half = tall // 2
        pass_y = shuffle(
            [gu_got[0], down_low],
            [(half + down_low.shape[0], width)],
            [(0, 0, 0, 0, 0, 0, half, width), (1, 0, 0, 0, half, 0, *down_low.shape)],
        )[0]
        pass_x = shuffle(
            [gu_got[1], down_low],
            [(half + down_low.shape[0], width)],
            [(0, half, 0, 0, 0, 0, half, width), (1, 0, 0, 0, half, 0, *down_low.shape)],
        )[0]
        passed = [give_to(pass_y, "y", 2, 1), give_to(pass_x, "x", X, 1)]
    else:
        passed = gather_first(down_low, y_count)
    ff_take, gu_rows, gu_got, down_low, passed = stage(ff_take, gu_rows, gu_got, down_low, passed)

    ff_rows = stack_rows(ff_take)
    ff_halves = [ff_rows, swap_core(ff_rows)]
    if y_count == 2:
        edge = down_low.shape[0] // 2
        down_far = [
            give_to(passed[1][half : half + edge], "y", 2, 1),
            give_to(passed[0][half + edge :], "x", X, 1),
        ]
        copies = []
        sources = [[(0, 0)], [(1, 0)], [(2, 0)], [(3, 0), (4, 0)]]
        for p in range(yx):
            for z in range(Z):
                part, low = sources[p][0] if p < 3 else sources[p][z * 2 // Z]
                low = z * unit if p < 3 else (z * unit) % half
                copies.append(
                    (part, low, 0, 0, (z * yx + places_yx[p], unit), 0, unit, width)
                )
        gu_mat = shuffle(
            [gu_rows, gu_got[0], gu_got[1], passed[0], passed[1]], [(Z * yx * unit, width)], copies
        )[0]
    else:
        down_far = passed
        gu_mat = place_parts(gu_rows, gu_got, [(0, 2 * ff_own)])[0]
    gate_proj, up_proj, hidden = [], [], []
    for part in ff_halves:
        gate_up = times(part, gu_mat)
        gate_proj.append(gate_up[:, :ff_own])
        up_proj.append(gate_up[:, ff_own:])
        hidden.append(glu_piece(gate_proj[-1], up_proj[-1]).astype(BF))
    hidden, down_far = stage(hidden, down_far)

    if y_count == 2:
        copies = [
            (0, 0, 0, 0, (places_yx[0], ff_shard), 0, ff_shard, width),
            (2, half, 0, 0, (places_yx[1], ff_shard), 0, ff_shard, width),
            (1, half, 0, 0, (places_yx[2], ff_shard), 0, ff_shard, width),
            (3, 0, 0, 0, (places_yx[3] * 2, edge), 0, edge, width),
            (4, 0, 0, 0, (places_yx[3] * 2 + 1, edge), 0, edge, width),
        ]
        down_mat = shuffle(
            [down_low, passed[0], passed[1], down_far[0], down_far[1]],
            [(yx * ff_shard, width)],
            copies,
        )[0]
    else:
        down_mat = place_blocks(down_low, down_far, ff_shard)
    down_share = times(hidden[1], down_mat)
    blocks = core_sum(times(hidden[0], down_mat), down_share)
    blocks, small_own, small_other = stage(blocks, small_own, small_other)
    shares = z_shares(blocks)

    def small_rows(value):
        value = value.reshape(-1, C, shard, ple)
        return jnp.concatenate([value[:, 0], value[:, 1]], axis=-1).reshape(-1, 2 * ple)

    ple_mat = core_rows(small_rows(small_own), small_rows(small_other))
    shares, ple_mat = stage(shares, ple_mat)
    pgate_mat, pproj_mat = ple_mat[:, :ple], ple_mat[:, ple:]
    down_proj = add_up(shares)

    extra_vals = layer_input[0].astype(F32)
    after_ff = joined + rms_norm(down_proj, gains[4])
    after_low = after_ff.astype(BF)
    per_gate = times(after_low, pgate_mat)
    per_mix = glu_piece(per_gate, extra_vals).astype(BF)
    per_out = times_t(per_mix, pproj_mat)
    d_output = cotangent[0].astype(F32)
    _, norm_pull = jax.vjp(rms_norm, per_out, gains[5])
    d_per_out, d_gain_ple = norm_pull(d_output)
    d_per_low = d_per_out.astype(BF)
    d_per_mix = times(d_per_low, pproj_mat)
    _, glu_pull = jax.vjp(glu_piece, per_gate, extra_vals)
    d_per_gate, d_extra = glu_pull(d_per_mix)
    d_pgate_low = d_per_gate.astype(BF)
    d_after = d_output + times_t(d_pgate_low, pgate_mat)
    _, norm_pull = jax.vjp(rms_norm, down_proj, gains[4])
    d_down, d_gain_post_ff = norm_pull(d_after)
    d_down_low = d_down.astype(BF)
    (
        d_down_low, after_late, d_pgate_late, d_per_late, per_mix_late, after_ff, per_out, d_gain_ple,
        d_gain_post_ff, d_extra,
    ) = stage(
        d_down_low, after_low, d_pgate_low, d_per_low, per_mix, after_ff, per_out, d_gain_ple,
        d_gain_post_ff, d_extra,
    )

    d_down_take = z_take(d_down_low)
    output = after_ff + rms_norm(per_out, gains[5])
    ple_grads = row_pieces(
        jnp.concatenate(
            [over_rows(after_late, d_pgate_late), over_rows(d_per_late, per_mix_late)], axis=1
        ).astype(BF)
    )
    ple_got = sum_first(ple_grads, y_count)
    d_down_take, ple_grads, ple_got = stage(d_down_take, ple_grads, ple_got)

    d_down_rows = stack_rows(d_down_take)
    d_down_halves = [d_down_rows, swap_core(d_down_rows)]
    ple_got = sum_second(ple_grads, list(ple_got), y_count)
    d_gu_low = []
    for h in range(C):
        d_hidden = times_t(d_down_halves[h], down_mat)
        _, glu_pull = jax.vjp(glu_piece, gate_proj[h], up_proj[h])
        d_gate, d_up = glu_pull(d_hidden)
        d_gu_low.append(jnp.concatenate([d_gate.astype(BF), d_up.astype(BF)], axis=-1))
    d_gu_low, ple_got = stage(d_gu_low, ple_got)

    term_share = times_t(d_gu_low[1], gu_mat)
    blocks = core_sum(times_t(d_gu_low[0], gu_mat), term_share)
    blocks, d_gu_low, ff_halves, hidden, d_down_halves = stage(
        blocks, d_gu_low, ff_halves, hidden, d_down_halves
    )
    share_mid = give_to(blocks[2], "z", Z, 2)

    def own_core(total):
        keep = jnp.where(first, total[:shard], total[shard:])
        send = jnp.where(first, total[shard:], total[:shard])
        return keep + swap_core(send.astype(BF)).astype(F32)

    def both_rows(lefts, rights):
        return (over_rows(lefts[0], rights[0]) + over_rows(lefts[1], rights[1])).astype(BF)

    gu_grads = [None] * yx
    down_grads = [None] * yx
    ff_pieces = column_pieces(ff_halves)

    def down_grad(p):
        return both_rows(
            [
                lax.dynamic_slice_in_dim(half_in, places_yx[p] * ff_shard, ff_shard, axis=1)
                for half_in in hidden
            ],
            d_down_halves,
        )

    gu_grads[yx - 1] = both_rows(ff_pieces[yx - 1], d_gu_low)
    down_grads[yx - 1] = down_grad(yx - 1)
    merged = [jnp.zeros((16, 128), BF)]
    if y_count == 2:
        merged = [
            shuffle(
                [gu_grads[3], down_grads[3]],
                [(half + edge, width)],
                [
                    (0, side * half, 0, 0, 0, 0, half, width),
                    (1, side * edge, 0, 0, half, 0, edge, width),
                ],
            )[0]
            for side in range(2)
        ]
    (
        share_mid, merged, blocks, ff_pieces, d_gu_low, hidden, d_down_halves, gu_grads[yx - 1],
        down_grads[yx - 1],
    ) = stage(
        share_mid, merged, blocks, ff_pieces, d_gu_low, hidden, d_down_halves, gu_grads[yx - 1],
        down_grads[yx - 1],
    )
    shares = [blocks[0], give_to(blocks[1], "z", Z, 1), give_to(blocks[3], "z", Z, 3), share_mid]
    if y_count == 2:
        merged_got = [give_to(merged[0], "x", X, 1), give_to(merged[1], "y", 2, 1)]
    for p in range(yx - 1):
        gu_grads[p] = both_rows(ff_pieces[p], d_gu_low)
        down_grads[p] = down_grad(p)
    if y_count != 2:
        merged_got = sum_first(gu_grads, y_count)
    shares, merged_got, gu_grads, down_grads = stage(shares, merged_got, gu_grads, down_grads)
    term = add_up(shares)
    if y_count == 2:
        gu_got = [got[:half] for got in merged_got]
        down_got = [got[half:] for got in merged_got]
    else:
        gu_got = list(merged_got)

    _, norm_pull = jax.vjp(rms_norm, joined, gains[3])
    d_joined_norm, d_gain_pre_ff = norm_pull(term)
    d_branch = (d_after + d_joined_norm) * HALF_ROOT
    _, norm_pull = jax.vjp(rms_norm, projected, gains[1])
    d_projected, d_gain_post_attn = norm_pull(d_branch)
    d_proj_low = d_projected.astype(BF)
    (
        d_proj_low, d_branch, d_gain_pre_ff, d_gain_post_attn, right_out, normed_own, normed_other
    ) = stage(
        d_proj_low, d_branch, d_gain_pre_ff, d_gain_post_attn, right_out, normed_own, normed_other
    )

    d_proj_take = z_take(d_proj_low)
    gu_got = sum_second(gu_grads, gu_got, y_count)
    _, norm_pull = jax.vjp(rms_norm, right_out, gains[2])
    d_right, d_gain_laurel = norm_pull(d_branch)
    d_right_low = d_right.astype(BF)
    d_left_low = times(d_right_low, right_mat).astype(BF)
    d_normed_own = d_branch + times_t(d_left_low, left_mat)
    left_grads = jnp.concatenate(
        [over_rows(d_left_low, normed_low), over_rows(left_low, d_right_low)], axis=0
    ).astype(BF)
    normed_pieces = column_pieces((normed_own, normed_other))
    d_proj_take, gu_got, left_grads, normed_pieces, d_normed_own = stage(
        d_proj_take, gu_got, left_grads, normed_pieces, d_normed_own
    )

    def by_core(rows_in, blocks):
        even = jnp.concatenate(
            [rows_in[2 * j * shard : (2 * j + 1) * shard] for j in range(blocks)], axis=0
        )
        odd = jnp.concatenate(
            [rows_in[(2 * j + 1) * shard : (2 * j + 2) * shard] for j in range(blocks)], axis=0
        )
        return jnp.where(first, even, odd), swap_core(jnp.where(first, odd, even))

    d_proj_rows = stack_rows(d_proj_take)
    d_proj_halves = [d_proj_rows, swap_core(d_proj_rows)]
    gu_sum = sum_total(gu_grads, gu_got).astype(BF)
    gu_pair = by_core(gu_sum, Z)
    gu_cores = [jnp.where(first, *gu_pair), jnp.where(first, *gu_pair[::-1])]
    ple_sum = sum_total(ple_grads, ple_got).astype(BF)
    ple_arrived = z_send(lambda k: z_block(ple_sum, k, unit))
    d_heads = jnp.concatenate([times_t(half_in, out_mat) for half_in in d_proj_halves], axis=0)
    d_heads, gu_cores, ple_arrived, d_proj_halves, down_grads = stage(
        d_heads, gu_cores, ple_arrived, d_proj_halves, down_grads
    )
    if y_count != 2:
        down_got = sum_first(down_grads, y_count)
    gu_arrived = [z_send(lambda k: z_block(gu_cores[0], k, shard))]
    down_got = sum_second(down_grads, down_got, y_count)
    d_heads = d_heads.astype(BF).reshape(C, group_rows, HD)
    delta = jnp.sum(d_heads.astype(F32) * head_out, axis=-1, keepdims=True)
    d_probs = jnp.einsum("sqd,skd->sqk", d_heads, value_all, preferred_element_type=F32)
    d_scores = (probs * (d_probs - delta)).astype(BF)
    d_query = jnp.einsum("sqk,skd->sqd", d_scores, key_all, preferred_element_type=F32)
    d_key = jnp.einsum("sqk,sqd->skd", d_scores, query, preferred_element_type=F32)
    d_value = jnp.einsum("sqk,sqd->skd", probs_low, d_heads, preferred_element_type=F32)
    d_key = d_key.reshape(C, y_count, group_rows, HD)
    d_value = d_value.reshape(C, y_count, group_rows, HD)

    def kv_share(stream):
        return jnp.concatenate([d_key[stream], d_value[stream]], axis=-1).reshape(-1, 2 * HD)

    kv_share_own, kv_share_other = kv_share(0), kv_share(1).astype(BF)
    (
        kv_share_own, kv_share_other, d_query, gu_arrived, gu_last, d_proj_halves, heads_low, down_got
    ) = stage(
        kv_share_own, kv_share_other, d_query, gu_arrived, gu_cores[1], d_proj_halves, heads_low,
        down_got,
    )

    kv_sum = kv_share_own + swap_core(kv_share_other).astype(F32)
    kv_sum = kv_sum.reshape(y_count, group_rows, 2 * HD)
    own_kv = kv_sum[0]
    for k in range(1, y_count):
        own_kv = own_kv + give_to(kv_sum[k].astype(BF), "y", y_count, k).astype(F32)
    gu_arrived = list(gu_arrived) + [z_send(lambda k: z_block(gu_last, k, shard))]
    _, rot_pull = jax.vjp(rotated, q_raw, qk[0])
    d_q_raw, d_gain_query = rot_pull(d_query.reshape(C * group_rows, HD))
    _, rot_pull = jax.vjp(rotated_own, k_raw[:group_rows], qk[1])
    d_k_raw, d_gain_key = rot_pull(own_kv[:, :HD])
    _, unit_pull = jax.vjp(unit_norm, v_raw[:group_rows])
    (d_v_raw,) = unit_pull(own_kv[:, HD:])
    d_q_low = d_q_raw.astype(BF)
    d_kv_low = jnp.concatenate([d_k_raw.astype(BF), d_v_raw.astype(BF)], axis=-1)
    d_own_low = jnp.concatenate([d_q_low[:group_rows], d_kv_low], axis=-1)
    d_q_low, d_kv_low, d_own_low, gu_arrived, down_grads, d_proj_halves = stage(
        d_q_low, d_kv_low, d_own_low, gu_arrived, down_grads, d_proj_halves
    )

    part_other = times_t(d_q_low[group_rows:], qkv_mat[:, :HD])
    part_own = times_t(d_own_low, qkv_mat)
    blocks = core_sum(part_own, part_other)
    blocks, part_own, part_other, d_q_low, d_kv_low, normed_pieces, left_grads = stage(
        blocks, part_own, part_other, d_q_low, d_kv_low, normed_pieces, left_grads
    )
    share_mid = give_to(blocks[2], "z", Z, 2)
    d_gain_input = (
        jnp.sum(part_own * unit_own, axis=0)
        + jnp.sum(part_other * unit_other, axis=0)
        + jnp.sum(d_normed_own * unit_norm(token_vals), axis=0)
    )
    d_qk = jnp.stack([d_gain_query, d_gain_key]).reshape(2, -1, qk_shard)
    d_qk = jnp.pad(d_qk, ((0, 0), (0, 0), (0, shard - qk_shard))).reshape(2, -1)
    gain_grads = jnp.stack(
        [d_gain_input, d_gain_post_attn, d_gain_laurel, d_gain_pre_ff, d_gain_post_ff, d_gain_ple]
    )
    gain_grads = jnp.concatenate([gain_grads, d_qk], axis=0)
    gain_grads = jnp.pad(gain_grads, ((0, 16 - gain_count - 2), (0, 0))).astype(BF)
    row_grads = jnp.concatenate([left_grads, gain_grads], axis=0)
    row_count = row_grads.shape[0]
    last_grads = []
    for p in range(yx):
        query_part = both_rows(normed_pieces[p], (d_q_low[:group_rows], d_q_low[group_rows:]))
        kv_part = over_rows(normed_pieces[p][0], d_kv_low).astype(BF)
        last_grads.append((query_part, kv_part))
    copies = []
    for p in range(yx):
        copies.append((C * p, 0, 0, p, 0, 0, tall, HD))
        copies.append((C * p + 1, 0, 0, p, 0, HD, tall, 2 * HD))
        for z in range(Z):
            column = (z * yx + places_yx[p], unit)
            copies.append((C * yx, 0, column, p, tall, z * unit, row_count, unit))
        copies.append((C * yx + 1, 0, 0, p, tall, tall, row_count, span - tall))
    last_grads = shuffle(
        [part for pair in last_grads for part in pair]
        + [row_grads, jnp.zeros((row_count, span - tall), BF)],
        [(tall + row_count, span)] * yx,
        copies,
    )
    share_mid, last_grads, blocks, heads_low, d_proj_halves, down_got, down_grads = stage(
        share_mid, last_grads, blocks, heads_low, d_proj_halves, down_got, down_grads
    )
    share_next = give_to(blocks[1], "z", Z, 1)
    last_got = sum_first(last_grads, y_count)
    out_grad = both_rows((heads_low[:group_rows], heads_low[group_rows:]), d_proj_halves)
    share_next, last_got, last_grads, out_grad, blocks, down_got, down_grads = stage(
        share_next, last_got, last_grads, out_grad, blocks, down_got, down_grads
    )
    shares = [blocks[0], share_mid, share_next, give_to(blocks[3], "z", Z, 3)]
    last_got = sum_second(last_grads, list(last_got), y_count)
    out_both = order_cores(*by_core(out_grad, yx // 2), first, 0)
    grad_down = sum_total(down_grads, down_got)
    shares, last_got, last_grads, out_both, gu_arrived, ple_arrived = stage(
        shares, last_got, last_grads, out_both, gu_arrived, ple_arrived
    )
    d_normed = d_normed_own + add_up(shares)

    last_low = sum_total(last_grads, last_got).astype(BF)
    qkv_pair = by_core(last_low[:tall], Z)
    qkv_cores = [jnp.where(first, *qkv_pair), jnp.where(first, *qkv_pair[::-1])]
    heights = [min(shard, row_count - low) for low in range(0, row_count, shard)]
    copies = []
    for k in range(Z):
        z_to = (zi + k) % Z
        for c in range(C):
            copies.append((c, (z_to, shard), 0, k, 0, c * span, shard, span))
        for j, height in enumerate(heights):
            copies.append(
                (2, tall + j * shard, (z_to, unit), k, 0, C * span + j * unit, height, unit)
            )
    last_sends = shuffle(
        qkv_cores + [last_low], [(shard, C * span + len(heights) * unit)] * Z, copies
    )
    last_sends, out_both, gu_arrived, ple_arrived, d_normed = stage(
        last_sends, out_both, gu_arrived, ple_arrived, d_normed
    )
    last_arrived = z_send(lambda k: last_sends[k])
    out_grads = [
        lax.dynamic_slice_in_dim(out_both, places_yx[p] * shard, shard) for p in range(yx)
    ]
    grad_out = sum_total(out_grads, sum_second(out_grads, sum_first(out_grads, y_count), y_count))
    ple_total = own_core(sum(piece.astype(F32) for piece in ple_arrived))
    _, norm_pull = jax.vjp(rms_norm, token_vals, gains[0])
    d_tokens_norm, _ = norm_pull(d_normed)
    d_tokens = d_branch + d_tokens_norm
    copies = []
    for k in range(Z):
        for c in range(C):
            for m in range(2):
                for a in range(yx):
                    column = (((zi - k) % Z * yx + a) * C + c, ff_shard)
                    copies.append(
                        (
                            c * Z + k, 0, m * ff_own + a * ff_shard,
                            m, 0, column, shard, ff_shard,
                        )
                    )
    grad_gu = shuffle(
        list(gu_arrived[0]) + list(gu_arrived[1]), [(shard, Z * yx * C * ff_shard)] * 2, copies
    )
    grad_gu = [grad.astype(F32) for grad in grad_gu]
    qkv_parts = z_place(last_arrived, zi)[:, : C * span].astype(F32)
    row_total = sum(piece[:, C * span :].astype(F32) for piece in last_arrived)
    row_total = jnp.concatenate(
        [row_total[:height, j * unit : (j + 1) * unit] for j, height in enumerate(heights)], axis=0
    )
    row_keep = jnp.where(first, row_total[:, :shard], row_total[:, shard:])
    row_send = jnp.where(first, row_total[:, shard:], row_total[:, :shard])
    row_total = row_keep + swap_core(row_send.astype(BF)).astype(F32)

    def qkv_part(z, c, m):
        return qkv_parts[z * shard : (z + 1) * shard, (3 * c + m) * HD : (3 * c + m + 1) * HD]

    grad_query = jnp.concatenate([qkv_part(z, c, 0) for z in range(Z) for c in range(C)], axis=1)
    grad_kv = [
        jnp.concatenate(
            [
                sum(
                    qkv_part(z, c, m)
                    for z in range(h * Z // KVH, (h + 1) * Z // KVH)
                    for c in range(C)
                )
                for h in range(KVH)
            ],
            axis=1,
        )
        for m in (1, 2)
    ]
    grad_gains = row_total[lanes : lanes + gain_count]
    grad_qk = row_total[lanes + gain_count : lanes + gain_count + 2, :qk_shard]
    return (
        output.astype(BF)[None],
        d_tokens.astype(BF)[None],
        d_extra.astype(BF)[None],
        grad_query,
        grad_kv[0],
        grad_kv[1],
        grad_out,
        row_total[:left_rank].T,
        row_total[left_rank:lanes],
        grad_gains,
        grad_qk,
        grad_gu[0],
        grad_gu[1],
        grad_down,
        ple_total[:, :ple],
        ple_total[:, ple:].T,
    )


def solution(mesh):
    fine = Mesh(mesh.devices.reshape(Z, -1, X, C), EVERY)
    rows = P(EVERY, None)
    cols = P(None, EVERY)
    stream = P(("x", "c"), ("z", "y"), None)
    return jax.shard_map(
        local,
        mesh=fine,
        in_specs=(
            stream, stream, stream, P(("x", "c"), None), P(),
            rows, rows, rows, rows, rows, cols, cols, cols, rows, rows, rows, rows, cols,
        ),
        out_specs=(
            stream, stream, stream,
            rows, rows, rows, rows, rows, cols, cols, cols, rows, rows, rows, rows, cols,
        ),
        check_vma=False,
    )
```

```python
import jax
import jax.numpy as jnp
from jax import lax
from jax.experimental import pallas as pl
from jax.experimental.pallas import tpu as pltpu
from jax.sharding import Mesh, PartitionSpec as P

H = 8
KVH = 2
HD = 256
Z = 4
X = 2
C = 2

EPSILON = 1e-06
ROPE_BASE = 1000000.0
HALF_ROOT = 0.7071067811865476
MASKED = -1e30
BF = jnp.bfloat16
F32 = jnp.float32
EVERY = ("z", "y", "x", "c")


def rms_norm(values_in, gain_in):
    return (
        values_in
        * lax.rsqrt(jnp.mean(values_in * values_in, axis=-1, keepdims=True) + EPSILON)
        * gain_in
    )


def unit_norm(values_in):
    return values_in * lax.rsqrt(
        jnp.mean(values_in * values_in, axis=-1, keepdims=True) + EPSILON
    )


def gelu_tanh(values_in):
    return jax.nn.gelu(values_in, approximate=True)


def glu_piece(gate_in, up_in):
    return gelu_tanh(gate_in) * up_in


def rotate(values_in, cos_tab, sine_tab):
    half_width = values_in.shape[-1] // 2
    first_half = values_in[..., :half_width]
    second_half = values_in[..., half_width:]
    return jnp.concatenate(
        [
            first_half * cos_tab - second_half * sine_tab,
            second_half * cos_tab + first_half * sine_tab,
        ],
        axis=-1,
    )


def times(left_in, right_in):
    return jnp.einsum("...a,ab->...b", left_in, right_in, preferred_element_type=F32)


def times_t(left_in, right_in):
    return jnp.einsum("...a,ba->...b", left_in, right_in, preferred_element_type=F32)


def over_rows(left_in, right_in):
    return jnp.einsum("ra,rb->ab", left_in, right_in, preferred_element_type=F32)


def give_to(value, axis, size, step):
    return lax.ppermute(value, axis, [(i, (i + step) % size) for i in range(size)])


def swap_core(value):
    return lax.ppermute(value, "c", [(0, 1), (1, 0)])


def after(value, *others):
    return lax.optimization_barrier((value, *others))[0]


def pick(value, index, axis):
    return lax.dynamic_index_in_dim(value, index, axis, keepdims=False)


def stage(*values):
    return lax.optimization_barrier(values)


def start_of(spec):
    return spec[0] * spec[1] if isinstance(spec, tuple) else spec


def shuffle(arrays, outs, copies):
    dtype = arrays[0].dtype
    aligned = True
    for _, r_in, c_in, _, r_out, c_out, height, wide in copies:
        for spec, tile in ((r_in, 16), (r_out, 16), (c_in, 128), (c_out, 128)):
            size = spec[1] if isinstance(spec, tuple) else spec
            aligned = aligned and size % tile == 0
        aligned = aligned and height % 16 == 0 and wide % 128 == 0
    if not aligned:
        made = [jnp.zeros(shape, dtype) for shape in outs]
        for a, r_in, c_in, o, r_out, c_out, height, wide in copies:
            piece = lax.dynamic_slice(
                arrays[a], (start_of(r_in), start_of(c_in)), (height, wide)
            )
            made[o] = lax.dynamic_update_slice(made[o], piece, (start_of(r_out), start_of(c_out)))
        return made
    numbers = []

    def known(spec):
        if not isinstance(spec, tuple):
            return spec
        numbers.append(spec[0])
        return (len(numbers) - 1, spec[1])

    plan = [
        (a, known(r_in), known(c_in), o, known(r_out), known(c_out), height, wide)
        for a, r_in, c_in, o, r_out, c_out, height, wide in copies
    ]
    table = jnp.stack([jnp.asarray(n, jnp.int32) for n in numbers] or [jnp.int32(0)])
    count = len(arrays)

    def kernel(table_ref, *refs):
        ins, made = refs[:count], refs[count:]

        def at(spec):
            if isinstance(spec, tuple):
                return pl.multiple_of(table_ref[spec[0]] * spec[1], spec[1])
            return spec

        for a, r_in, c_in, o, r_out, c_out, height, wide in plan:
            from_row, from_column, to_row, to_column = at(r_in), at(c_in), at(r_out), at(c_out)
            step = 16
            while height % (2 * step) == 0 and 2 * step * wide <= 65536:
                step *= 2
            chunks = height // step

            def move(low):
                made[o][pl.ds(to_row + low, step), pl.ds(to_column, wide)] = ins[a][
                    pl.ds(from_row + low, step), pl.ds(from_column, wide)
                ]

            if chunks % 4 or chunks <= 8:
                for i in range(chunks):
                    move(i * step)
            else:

                @pl.loop(0, chunks // 4)
                def _(i):
                    for j in range(4):
                        move(pl.multiple_of(i * 4 * step, step) + j * step)

    moved = sum(height * wide for *_, height, wide in plan) * dtype.itemsize
    return pl.pallas_call(
        kernel,
        out_shape=[jax.ShapeDtypeStruct(shape, dtype) for shape in outs],
        grid_spec=pltpu.PrefetchScalarGridSpec(
            num_scalar_prefetch=1,
            grid=(1,),
            in_specs=[pl.BlockSpec(memory_space=pltpu.VMEM)] * count,
            out_specs=[pl.BlockSpec(memory_space=pltpu.VMEM)] * len(outs),
        ),
        cost_estimate=pl.CostEstimate(flops=0, bytes_accessed=2 * moved, transcendentals=0),
    )(table, *arrays)


def stack_rows(pieces):
    if len(pieces) == 1:
        return pieces[0]
    copies = []
    low = 0
    for i, piece in enumerate(pieces):
        copies.append((i, 0, 0, 0, low, 0, *piece.shape))
        low += piece.shape[0]
    return shuffle(pieces, [(low, pieces[0].shape[1])], copies)[0]


def z_take(block):
    return [block if k == 0 else give_to(block, "z", Z, -k) for k in range(Z)]


def flat_step(step_y, step_x, y_count):
    return [
        (y * X + x, ((y + step_y) % y_count) * X + (x + step_x) % X)
        for y in range(y_count)
        for x in range(X)
    ]


def all_steps(y_count):
    return [(p // X, p % X) for p in range(1, y_count * X)]


def gather_first(block, y_count):
    if y_count == 2:
        return [give_to(block, "x", X, 1), give_to(block, "y", 2, 1)]
    return [
        lax.ppermute(block, ("y", "x"), flat_step(-dy, -dx, y_count)) for dy, dx in all_steps(y_count)
    ]


def gather_second(block, got, y_count):
    if y_count == 2:
        half = block.shape[0] // 2
        return got + [give_to(got[0][:half], "y", 2, 1), give_to(got[1][half:], "x", X, 1)]
    return got


def gather_parts(block, got, y_count):
    arrays = [block] + list(got)
    rows = block.shape[0]
    parts = [[(i, 0, rows)] for i in range(len(arrays))]
    if y_count == 2:
        parts = parts[:3] + [[(3, 0, rows // 2), (4, 0, rows // 2)]]
    return arrays, parts


def sum_first(pieces, y_count):
    if y_count == 2:
        half = pieces[3].shape[0] // 2
        return [give_to(pieces[3][:half], "x", X, 1), give_to(pieces[3][half:], "y", 2, 1)]
    return [
        lax.ppermute(pieces[dy * X + dx], ("y", "x"), flat_step(dy, dx, y_count))
        for dy, dx in all_steps(y_count)
    ]


def add_low(first_in, second_in):
    return (first_in.astype(F32) + second_in.astype(F32)).astype(BF)


def sum_second(pieces, got, y_count):
    if y_count == 2:
        half = pieces[3].shape[0] // 2
        to_y = jnp.concatenate([add_low(pieces[2][:half], got[0]), pieces[2][half:]], axis=0)
        to_x = jnp.concatenate([pieces[1][:half], add_low(pieces[1][half:], got[1])], axis=0)
        return [give_to(to_y, "y", 2, 1), give_to(to_x, "x", X, 1)]
    return got


def sum_total(pieces, got):
    return add_up([pieces[0]] + list(got))


def core_sum(own, other):
    total = own + swap_core(other.astype(BF)).astype(F32)
    rows = total.shape[0] // Z
    return [total[:rows]] + [
        total[k * rows : (k + 1) * rows].astype(BF) for k in range(1, Z)
    ]


def z_shares(blocks):
    return [blocks[0]] + [give_to(blocks[k], "z", Z, k) for k in range(1, Z)]


def add_up(pieces):
    total = pieces[0].astype(F32)
    for piece in pieces[1:]:
        total = total + piece.astype(F32)
    return total


def write_rows(pieces, starts):
    rows, width = pieces[0].shape
    whole = jnp.zeros((rows * len(pieces), width), pieces[0].dtype)
    for piece, start in zip(pieces, starts):
        whole = lax.dynamic_update_slice_in_dim(whole, piece, start, 0)
    return whole


def z_send(sends):
    return [sends(k) if k == 0 else give_to(sends(k), "z", Z, k) for k in range(Z)]


def z_place(arrived, zi):
    rows, width = arrived[0].shape
    copies = [(k, 0, 0, 0, ((zi - k) % Z, rows), 0, rows, width) for k in range(Z)]
    return shuffle(arrived, [(Z * rows, width)], copies)[0]


def order_cores(own, other, first, axis):
    return jnp.concatenate(
        [jnp.where(first, own, other), jnp.where(first, other, own)], axis=axis
    )


def places(pair_of, lengths, ctx_ids, row_count):
    blocks_last = 2 * pair_of.shape[0] - 1
    half_rows = row_count // 2
    pair = pair_of[ctx_ids][:, None]
    row = jnp.arange(row_count, dtype=jnp.int32)[None, :]
    block = jnp.where(row < half_rows, pair, blocks_last - pair)
    position = (block * half_rows + row % half_rows).reshape(-1)
    ends = jnp.cumsum(lengths, dtype=jnp.int32)
    before = ends[None, :] <= position[:, None]
    segment = jnp.sum(before.astype(jnp.int32), axis=1, dtype=jnp.int32)
    start = jnp.sum(jnp.where(before, lengths[None, :], 0), axis=1, dtype=jnp.int32)
    return position, segment, position - start


def local(
    tokens,
    layer_input,
    cotangent,
    doc_lengths,
    pair_of,
    w_query,
    w_key,
    w_value,
    w_out,
    w_left,
    w_right,
    norm_gains,
    qk_gain,
    w_gate,
    w_up,
    w_down,
    w_pgate,
    w_pproj,
):
    rows = tokens.shape[1]
    width = tokens.shape[2]
    y_count = lax.axis_size("y")
    zi, yi, xi, ci = (lax.axis_index(name) for name in EVERY)
    first = ci == 0
    shard = w_query.shape[0]
    ff_shard = w_down.shape[0]
    yx = y_count * X
    unit = C * shard
    places_yx = [((yi + p // X) % y_count) * X + (xi + p % X) % X for p in range(yx)]
    tall = Z * unit

    def place_parts(block, got, cuts):
        arrays, parts = gather_parts(block, got, y_count)
        copies = []
        for p in range(yx):
            z = 0
            for i, _, height in parts[p]:
                for low in range(0, height, unit):
                    to = (z * yx + places_yx[p], unit)
                    for o, (left_edge, right_edge) in enumerate(cuts):
                        copies.append(
                            (i, low, left_edge, o, to, 0, unit, right_edge - left_edge)
                        )
                    z += 1
        outs = [(Z * yx * unit, high - low) for low, high in cuts]
        return shuffle(arrays, outs, copies)

    def place_blocks(block, got, height):
        arrays, parts = gather_parts(block, got, y_count)
        copies = []
        for p in range(yx):
            low = 0
            for i, _, part in parts[p]:
                to = (places_yx[p] * (height // part) + low // part, part)
                copies.append((i, 0, 0, 0, to, 0, part, block.shape[1]))
                low += part
        return shuffle(arrays, [(yx * height, block.shape[1])], copies)[0]

    def row_pieces(value):
        value = value.reshape(Z, yx, unit, -1)
        return [pick(value, places_yx[p], 1).reshape(tall, -1) for p in range(yx)]

    def column_pieces(halves):
        copies = []
        for p in range(yx):
            for h in range(C):
                for z in range(Z):
                    column = (z * yx + places_yx[p], unit)
                    copies.append(
                        (h, 0, column, p * C + h, 0, z * unit, halves[h].shape[0], unit)
                    )
        made = shuffle(list(halves), [(halves[0].shape[0], tall)] * (C * yx), copies)
        return [made[p * C : p * C + C] for p in range(yx)]

    def pair_cores(own, height):
        other = swap_core(own)
        last = own.shape[1]
        cores = [jnp.where(first, own, other), jnp.where(first, other, own)]
        return jnp.concatenate([core.reshape(-1, 1, height, last) for core in cores], axis=1)

    left_rank = w_left.shape[1]
    ple = w_pgate.shape[1]
    gain_count = norm_gains.shape[0]
    qk_shard = qk_gain.shape[1]
    ff_own = yx * ff_shard
    lanes = 2 * left_rank
    span = 3 * HD

    group_rows = Z * rows

    def z_block(value, k, height, axis=0):
        return lax.dynamic_slice_in_dim(value, (zi + k) % Z * height, height, axis=axis)

    gain_pack = jnp.concatenate(
        [
            jnp.pad(norm_gains, ((0, 0), (0, lanes - shard))),
            jnp.pad(qk_gain, ((0, 0), (0, lanes - qk_shard))),
        ],
        axis=0,
    )
    gain_rows = gain_count + 2
    qkv_low = jnp.concatenate(
        [w_query, w_key, w_value, jnp.pad(gain_pack, ((0, shard - gain_rows), (0, 0)))], axis=1
    ).astype(BF)
    qkv_got = swap_core(qkv_low)
    qkv_low, qkv_got, out_late = stage(qkv_low, qkv_got, w_out)

    gain_low = (H + 2 * KVH) * HD
    own_gain, other_gain = qkv_low[:gain_rows, gain_low:], qkv_got[:gain_rows, gain_low:]
    gain_block = jnp.concatenate(
        [
            jnp.where(first, own_gain, other_gain),
            jnp.where(first, other_gain, own_gain),
            jnp.zeros((max(shard - C * gain_rows, 0), lanes), BF),
        ],
        axis=0,
    )[:shard]
    misc = jnp.concatenate(
        [
            jnp.concatenate([w_left, w_right.T, w_pgate], axis=1).astype(BF),
            jnp.concatenate([gain_block, w_pproj.T.astype(BF)], axis=1),
        ],
        axis=0,
    )
    copies = []
    for k in range(Z):
        z_to = (zi + k) % Z
        head = z_to * KVH // Z
        columns = [z_to * C + ci, H + head, H + KVH + head]
        for a, c_from in ((0, ci), (1, 1 - ci)):
            for j, column in enumerate(columns):
                copies.append((a, 0, (column, HD), k, (c_from, shard), j * HD, shard, HD))
        copies.append((2, 0, 0, k, 0, span, unit, misc.shape[1]))
    first_sends = shuffle(
        [qkv_low, qkv_got, misc], [(unit, span + misc.shape[1])] * Z, copies
    )
    first_arrived = z_send(lambda k: first_sends[k])
    gate_late, up_late, out_late, _ = stage(w_gate, w_up, out_late, first_sends)
    ff_low = jnp.concatenate([gate_late, up_late], axis=1).astype(BF)
    ff_got = swap_core(ff_low)
    out_low = out_late.astype(BF)
    out_x = give_to(out_low, "x", X, 1) if y_count == 2 else out_low
    own_tokens, pair_of, first_arrived, ff_low, ff_got, out_low, out_x = stage(
        tokens[0], pair_of, first_arrived, ff_low, ff_got, out_low, out_x
    )

    token_take = z_take(own_tokens)
    first_rows = z_place(first_arrived, zi)
    first_got = gather_first(first_rows, y_count)
    copies = []
    for m in range(2):
        for k in range(Z):
            for a in range(yx):
                part, low = divmod(a, yx // 2)
                for source, c_from in ((0, ci), (1, 1 - ci)):
                    column = (((m * Z + (zi + k) % Z) * yx + a) * C + ci, ff_shard)
                    copies.append(
                        (
                            source, 0, column, (2 * m + part) * Z + k, (c_from, shard),
                            low * ff_shard, shard, ff_shard,
                        )
                    )
    ff_sends = shuffle([ff_low, ff_got], [(unit, ff_own // 2)] * (4 * Z), copies)
    ff_sends = [ff_sends[j * Z : (j + 1) * Z] for j in range(4)]
    out_pair = stack_rows([out_low, out_x])
    first_rows, first_got = stage(first_rows, first_got)
    first_got = gather_second(first_rows, list(first_got), y_count)

    lengths = [doc_lengths[0], swap_core(doc_lengths)[0]]
    z_ids = (zi + jnp.arange(Z)) % Z
    own_ids = z_ids * y_count + yi
    key_ids = (z_ids[None, :] * y_count + ((yi + jnp.arange(y_count)) % y_count)[:, None]).reshape(-1)
    visible = []
    relative = []
    for lens in lengths:
        q_pos, q_seg, q_rel = places(pair_of, lens, own_ids, rows)
        k_pos, k_seg, _ = places(pair_of, lens, key_ids, rows)
        seen = (k_seg[None, :] == q_seg[:, None]) & (k_pos[None, :] <= q_pos[:, None])
        visible.append(seen.astype(F32))
        relative.append(q_rel)
    visible = jnp.stack(visible)
    relative = jnp.concatenate(relative)
    frequency = ROPE_BASE ** (-2.0 * jnp.arange(HD // 2, dtype=F32) / HD)
    angles = relative.astype(F32)[:, None] * frequency[None, :]
    cos_tab, sine_tab = jnp.cos(angles), jnp.sin(angles)
    (
        token_take, first_rows, first_got, ff_sends, visible, cos_tab, sine_tab, out_pair
    ) = stage(
        token_take, first_rows, first_got, ff_sends, visible, cos_tab, sine_tab, out_pair
    )
    visible = visible > 0.5

    def rotated(raw_in, gain_in):
        return rotate(rms_norm(raw_in, gain_in), cos_tab, sine_tab)

    def rotated_own(raw_in, gain_in):
        return rotate(rms_norm(raw_in, gain_in), cos_tab[:group_rows], sine_tab[:group_rows])

    token_own = stack_rows(token_take)
    token_other = swap_core(token_own)
    ff_arrived = [z_send(lambda k: ff_sends[0][k])]
    qkv_mat, misc_all, small_late = place_parts(
        first_rows,
        first_got,
        [(0, span), (span, span + lanes), (span + lanes, span + lanes + ple)],
    )
    gain_all = misc_all.reshape(-1, unit, lanes)[:, shard : shard + C * gain_rows, :shard]
    gain_all = gain_all.reshape(-1, gain_rows, shard).transpose(1, 0, 2)
    gains = gain_all[:gain_count].reshape(gain_count, -1).astype(F32)
    qk = gain_all[gain_count:, :, :qk_shard].reshape(2, -1).astype(F32)
    lr_own = misc_all.reshape(-1, unit, lanes)[:, :shard].reshape(-1, lanes)
    unit_own = unit_norm(token_own.astype(F32))
    unit_other = unit_norm(token_other.astype(F32))
    normed_own = (unit_own * gains[0]).astype(BF)
    normed_other = (unit_other * gains[0]).astype(BF)
    qkv = jnp.concatenate([times(normed_own, qkv_mat), times(normed_other, qkv_mat)], axis=0)
    q_raw, k_raw, v_raw = qkv[:, :HD], qkv[:, HD : 2 * HD], qkv[:, 2 * HD :]
    query = rotated(q_raw, qk[0]).astype(BF).reshape(C, group_rows, HD)
    key = rotated(k_raw, qk[1]).astype(BF)
    value = unit_norm(v_raw).astype(BF)
    kv = jnp.concatenate([key, value], axis=-1).reshape(C, group_rows, 2 * HD)
    out_y = give_to(out_pair, "y", 2, 1) if y_count == 2 else out_pair
    kv, query, ff_arrived, ff_sends, out_pair, out_y, lr_own, small_own = stage(
        kv, query, ff_arrived, ff_sends, out_pair, out_y, lr_own, small_late
    )
    ff_arrived = list(ff_arrived) + [z_send(lambda k: ff_sends[1][k])]

    kv_own = [kv[0]] + [give_to(kv[0], "y", y_count, -k) for k in range(1, y_count)]
    if y_count == 2:
        copies = []
        for p in range(yx):
            copies.append(
                (p // X, p % X * shard, 0, 0, (places_yx[p], shard), 0, shard, width)
            )
        out_rows = shuffle([out_pair, out_y], [(yx * shard, width)], copies)[0]
        out_half = yx // 2 * shard
        out_got = swap_core(lax.dynamic_slice_in_dim(out_rows, (1 - ci) * out_half, out_half))
    else:
        out_rows = lax.all_gather(out_pair[:shard], ("y", "x", "c"), axis=0, tiled=True)
        out_got = out_rows
    kv_own, ff_arrived, ff_sends, out_rows, out_got = stage(
        kv_own, ff_arrived, ff_sends, out_rows, out_got
    )

    if y_count == 2:
        copies = []
        for a in range(yx // 2):
            copies.append(
                (0, (ci * (yx // 2) + a, shard), 0, 0, (a * C + ci, shard), 0, shard, width)
            )
            copies.append((1, a * shard, 0, 0, (a * C + 1 - ci, shard), 0, shard, width))
        out_mat = shuffle([out_rows, out_got], [(HD, width)], copies)[0]
    else:
        out_mat = lax.dynamic_slice_in_dim(out_rows, ci * HD, HD)
    ff_arrived = list(ff_arrived) + [z_send(lambda k: ff_sends[2][k])]
    kv_other = [kv[1]] + [swap_core(piece) for piece in kv_own[1:]]
    kv_all = jnp.stack([jnp.concatenate(kv_own), jnp.concatenate(kv_other)])
    key_all, value_all = kv_all[..., :HD], kv_all[..., HD:]
    scores = jnp.einsum("sqd,skd->sqk", query, key_all, preferred_element_type=F32)
    scores = jnp.where(visible, scores, MASKED)
    top = jnp.max(scores, axis=-1, keepdims=True)
    log_total = top + jnp.log(jnp.sum(jnp.exp(scores - top), axis=-1, keepdims=True))
    probs = jnp.exp(scores - log_total)
    probs_low = probs.astype(BF)
    head_out = jnp.einsum("sqk,skd->sqd", probs_low, value_all, preferred_element_type=F32)
    heads_low = head_out.astype(BF).reshape(C * group_rows, HD)
    heads_low, ff_arrived, ff_sends, out_mat, lr_own = stage(
        heads_low, ff_arrived, ff_sends, out_mat, lr_own
    )

    heads_share = times(heads_low[group_rows:], out_mat)
    ff_arrived = list(ff_arrived) + [z_send(lambda k: ff_sends[3][k])]
    lr_other = swap_core(lr_own)
    blocks = core_sum(times(heads_low[:group_rows], out_mat), heads_share)
    blocks, ff_arrived, lr_own, lr_other, own_tokens, heads_low = stage(
        blocks, ff_arrived, lr_own, lr_other, own_tokens, heads_low
    )
    copies = [
        (j * Z + k, 0, 0, 0, ((zi - k) % Z, unit), j * (ff_own // 2), unit, ff_own // 2)
        for j in range(4)
        for k in range(Z)
    ]
    gu_rows = shuffle(
        [piece for pieces in ff_arrived for piece in pieces], [(tall, 2 * ff_own)], copies
    )[0]
    shares = z_shares(blocks)
    gu_got = gather_first(gu_rows, y_count)

    def core_rows(own, other):
        last = own.shape[1]
        cores = [jnp.where(first, own, other), jnp.where(first, other, own)]
        return jnp.concatenate(
            [core.reshape(-1, 1, shard, last) for core in cores], axis=1
        ).reshape(-1, last)

    lr_mat = core_rows(lr_own, lr_other)
    left_mat, right_mat = lr_mat[:, :left_rank], lr_mat[:, left_rank:]
    token_vals = own_tokens.astype(F32)
    normed = rms_norm(token_vals, gains[0])
    normed_low = normed.astype(BF)
    left_low = times(normed_low, left_mat).astype(BF)
    right_out = times_t(left_low, right_mat)
    laurel = normed + rms_norm(right_out, gains[2])
    shares, gu_rows, gu_got, laurel, w_down = stage(shares, gu_rows, gu_got, laurel, w_down)

    projected = add_up(shares)
    gated_sum = token_vals + rms_norm(projected, gains[1])
    joined = (gated_sum + laurel) * HALF_ROOT
    ff_in = rms_norm(joined, gains[3]).astype(BF)
    ff_in, gu_got, gu_rows, w_down = stage(ff_in, gu_got, gu_rows, w_down)
    ff_take = z_take(ff_in)
    down_low = w_down.astype(BF)
    if y_count == 2:
        half = tall // 2
        pass_y = shuffle(
            [gu_got[0], down_low],
            [(half + down_low.shape[0], width)],
            [(0, 0, 0, 0, 0, 0, half, width), (1, 0, 0, 0, half, 0, *down_low.shape)],
        )[0]
        pass_x = shuffle(
            [gu_got[1], down_low],
            [(half + down_low.shape[0], width)],
            [(0, half, 0, 0, 0, 0, half, width), (1, 0, 0, 0, half, 0, *down_low.shape)],
        )[0]
        passed = [give_to(pass_y, "y", 2, 1), give_to(pass_x, "x", X, 1)]
    else:
        passed = gather_first(down_low, y_count)
    ff_take, gu_rows, gu_got, down_low, passed = stage(ff_take, gu_rows, gu_got, down_low, passed)

    ff_rows = stack_rows(ff_take)
    ff_halves = [ff_rows, swap_core(ff_rows)]
    if y_count == 2:
        edge = down_low.shape[0] // 2
        down_far = [
            give_to(passed[1][half : half + edge], "y", 2, 1),
            give_to(passed[0][half + edge :], "x", X, 1),
        ]
        copies = []
        sources = [[(0, 0)], [(1, 0)], [(2, 0)], [(3, 0), (4, 0)]]
        for p in range(yx):
            for z in range(Z):
                part, low = sources[p][0] if p < 3 else sources[p][z * 2 // Z]
                low = z * unit if p < 3 else (z * unit) % half
                copies.append(
                    (part, low, 0, 0, (z * yx + places_yx[p], unit), 0, unit, width)
                )
        gu_mat = shuffle(
            [gu_rows, gu_got[0], gu_got[1], passed[0], passed[1]], [(Z * yx * unit, width)], copies
        )[0]
    else:
        down_far = passed
        gu_mat = place_parts(gu_rows, gu_got, [(0, 2 * ff_own)])[0]
    gate_proj, up_proj, hidden = [], [], []
    for part in ff_halves:
        gate_up = times(part, gu_mat)
        gate_proj.append(gate_up[:, :ff_own])
        up_proj.append(gate_up[:, ff_own:])
        hidden.append(glu_piece(gate_proj[-1], up_proj[-1]).astype(BF))
    hidden, down_far, small_own = stage(hidden, down_far, small_own)

    if y_count == 2:
        copies = [
            (0, 0, 0, 0, (places_yx[0], ff_shard), 0, ff_shard, width),
            (2, half, 0, 0, (places_yx[1], ff_shard), 0, ff_shard, width),
            (1, half, 0, 0, (places_yx[2], ff_shard), 0, ff_shard, width),
            (3, 0, 0, 0, (places_yx[3] * 2, edge), 0, edge, width),
            (4, 0, 0, 0, (places_yx[3] * 2 + 1, edge), 0, edge, width),
        ]
        down_mat = shuffle(
            [down_low, passed[0], passed[1], down_far[0], down_far[1]],
            [(yx * ff_shard, width)],
            copies,
        )[0]
    else:
        down_mat = place_blocks(down_low, down_far, ff_shard)
    down_share = times(hidden[1], down_mat)
    small_other = swap_core(small_own)
    blocks = core_sum(times(hidden[0], down_mat), down_share)
    blocks, small_own, small_other = stage(blocks, small_own, small_other)
    shares = z_shares(blocks)

    def small_rows(value):
        value = value.reshape(-1, C, shard, ple)
        return jnp.concatenate([value[:, 0], value[:, 1]], axis=-1).reshape(-1, 2 * ple)

    ple_mat = core_rows(small_rows(small_own), small_rows(small_other))
    shares, ple_mat = stage(shares, ple_mat)
    pgate_mat, pproj_mat = ple_mat[:, :ple], ple_mat[:, ple:]
    down_proj = add_up(shares)

    extra_vals = layer_input[0].astype(F32)
    after_ff = joined + rms_norm(down_proj, gains[4])
    after_low = after_ff.astype(BF)
    per_gate = times(after_low, pgate_mat)
    per_mix = glu_piece(per_gate, extra_vals).astype(BF)
    per_out = times_t(per_mix, pproj_mat)
    d_output = cotangent[0].astype(F32)
    _, norm_pull = jax.vjp(rms_norm, per_out, gains[5])
    d_per_out, d_gain_ple = norm_pull(d_output)
    d_per_low = d_per_out.astype(BF)
    d_per_mix = times(d_per_low, pproj_mat)
    _, glu_pull = jax.vjp(glu_piece, per_gate, extra_vals)
    d_per_gate, d_extra = glu_pull(d_per_mix)
    d_pgate_low = d_per_gate.astype(BF)
    d_after = d_output + times_t(d_pgate_low, pgate_mat)
    _, norm_pull = jax.vjp(rms_norm, down_proj, gains[4])
    d_down, d_gain_post_ff = norm_pull(d_after)
    d_down_low = d_down.astype(BF)
    (
        d_down_low, after_late, d_pgate_late, d_per_late, per_mix_late, after_ff, per_out, d_gain_ple,
        d_gain_post_ff, d_extra,
    ) = stage(
        d_down_low, after_low, d_pgate_low, d_per_low, per_mix, after_ff, per_out, d_gain_ple,
        d_gain_post_ff, d_extra,
    )

    d_down_take = z_take(d_down_low)
    output = after_ff + rms_norm(per_out, gains[5])
    ple_grads = row_pieces(
        jnp.concatenate(
            [over_rows(after_late, d_pgate_late), over_rows(d_per_late, per_mix_late)], axis=1
        ).astype(BF)
    )
    ple_got = sum_first(ple_grads, y_count)
    d_down_take, ple_grads, ple_got = stage(d_down_take, ple_grads, ple_got)

    d_down_rows = stack_rows(d_down_take)
    d_down_halves = [d_down_rows, swap_core(d_down_rows)]
    ple_got = sum_second(ple_grads, list(ple_got), y_count)
    d_gu_low = []
    for h in range(C):
        d_hidden = times_t(d_down_halves[h], down_mat)
        _, glu_pull = jax.vjp(glu_piece, gate_proj[h], up_proj[h])
        d_gate, d_up = glu_pull(d_hidden)
        d_gu_low.append(jnp.concatenate([d_gate.astype(BF), d_up.astype(BF)], axis=-1))
    d_gu_low, ple_got = stage(d_gu_low, ple_got)

    term_share = times_t(d_gu_low[1], gu_mat)
    ple_sum = sum_total(ple_grads, ple_got).astype(BF)
    ple_arrived = z_send(lambda k: z_block(ple_sum, k, unit))
    blocks = core_sum(times_t(d_gu_low[0], gu_mat), term_share)
    blocks, d_gu_low, ff_halves, hidden, d_down_halves, ple_arrived = stage(
        blocks, d_gu_low, ff_halves, hidden, d_down_halves, ple_arrived
    )
    share_mid = give_to(blocks[2], "z", Z, 2)

    def own_core(total):
        keep = jnp.where(first, total[:shard], total[shard:])
        send = jnp.where(first, total[shard:], total[:shard])
        return keep + swap_core(send.astype(BF)).astype(F32)

    def both_rows(lefts, rights):
        return (over_rows(lefts[0], rights[0]) + over_rows(lefts[1], rights[1])).astype(BF)

    gu_grads = [None] * yx
    down_grads = [None] * yx
    ff_pieces = column_pieces(ff_halves)

    def down_grad(p):
        return both_rows(
            [
                lax.dynamic_slice_in_dim(half_in, places_yx[p] * ff_shard, ff_shard, axis=1)
                for half_in in hidden
            ],
            d_down_halves,
        )

    gu_grads[yx - 1] = both_rows(ff_pieces[yx - 1], d_gu_low)
    down_grads[yx - 1] = down_grad(yx - 1)
    merged = [jnp.zeros((16, 128), BF)]
    if y_count == 2:
        merged = [
            shuffle(
                [gu_grads[3], down_grads[3]],
                [(half + edge, width)],
                [
                    (0, side * half, 0, 0, 0, 0, half, width),
                    (1, side * edge, 0, 0, half, 0, edge, width),
                ],
            )[0]
            for side in range(2)
        ]
    (
        share_mid, merged, blocks, ff_pieces, d_gu_low, hidden, d_down_halves, gu_grads[yx - 1],
        down_grads[yx - 1],
    ) = stage(
        share_mid, merged, blocks, ff_pieces, d_gu_low, hidden, d_down_halves, gu_grads[yx - 1],
        down_grads[yx - 1],
    )
    shares = [blocks[0], give_to(blocks[1], "z", Z, 1), give_to(blocks[3], "z", Z, 3), share_mid]
    if y_count == 2:
        merged_got = [give_to(merged[0], "x", X, 1), give_to(merged[1], "y", 2, 1)]
    for p in range(yx - 1):
        gu_grads[p] = both_rows(ff_pieces[p], d_gu_low)
        down_grads[p] = down_grad(p)
    if y_count != 2:
        merged_got = sum_first(gu_grads, y_count)
    shares, merged_got, gu_grads, down_grads = stage(shares, merged_got, gu_grads, down_grads)
    term = add_up(shares)
    if y_count == 2:
        gu_got = [got[:half] for got in merged_got]
        down_got = [got[half:] for got in merged_got]
    else:
        gu_got = list(merged_got)

    _, norm_pull = jax.vjp(rms_norm, joined, gains[3])
    d_joined_norm, d_gain_pre_ff = norm_pull(term)
    d_branch = (d_after + d_joined_norm) * HALF_ROOT
    _, norm_pull = jax.vjp(rms_norm, projected, gains[1])
    d_projected, d_gain_post_attn = norm_pull(d_branch)
    d_proj_low = d_projected.astype(BF)
    (
        d_proj_low, d_branch, d_gain_pre_ff, d_gain_post_attn, right_out, normed_own, normed_other
    ) = stage(
        d_proj_low, d_branch, d_gain_pre_ff, d_gain_post_attn, right_out, normed_own, normed_other
    )

    d_proj_take = z_take(d_proj_low)
    gu_got = sum_second(gu_grads, gu_got, y_count)
    _, norm_pull = jax.vjp(rms_norm, right_out, gains[2])
    d_right, d_gain_laurel = norm_pull(d_branch)
    d_right_low = d_right.astype(BF)
    d_left_low = times(d_right_low, right_mat).astype(BF)
    d_normed_own = d_branch + times_t(d_left_low, left_mat)
    left_grads = jnp.concatenate(
        [over_rows(d_left_low, normed_low), over_rows(left_low, d_right_low)], axis=0
    ).astype(BF)
    normed_pieces = column_pieces((normed_own, normed_other))
    d_proj_take, gu_got, left_grads, normed_pieces, d_normed_own = stage(
        d_proj_take, gu_got, left_grads, normed_pieces, d_normed_own
    )

    def by_core(rows_in, blocks):
        even = jnp.concatenate(
            [rows_in[2 * j * shard : (2 * j + 1) * shard] for j in range(blocks)], axis=0
        )
        odd = jnp.concatenate(
            [rows_in[(2 * j + 1) * shard : (2 * j + 2) * shard] for j in range(blocks)], axis=0
        )
        return jnp.where(first, even, odd), swap_core(jnp.where(first, odd, even))

    d_proj_rows = stack_rows(d_proj_take)
    d_proj_halves = [d_proj_rows, swap_core(d_proj_rows)]
    gu_sum = sum_total(gu_grads, gu_got).astype(BF)
    gu_pair = by_core(gu_sum, Z)
    gu_cores = [jnp.where(first, *gu_pair), jnp.where(first, *gu_pair[::-1])]
    d_heads = jnp.concatenate([times_t(half_in, out_mat) for half_in in d_proj_halves], axis=0)
    if y_count != 2:
        down_got = sum_first(down_grads, y_count)
    gu_arrived = [z_send(lambda k: z_block(gu_cores[0], k, shard))]
    down_got = sum_second(down_grads, down_got, y_count)
    d_heads = d_heads.astype(BF).reshape(C, group_rows, HD)
    delta = jnp.sum(d_heads.astype(F32) * head_out, axis=-1, keepdims=True)
    d_probs = jnp.einsum("sqd,skd->sqk", d_heads, value_all, preferred_element_type=F32)
    d_scores = (probs * (d_probs - delta)).astype(BF)
    d_query = jnp.einsum("sqk,skd->sqd", d_scores, key_all, preferred_element_type=F32)
    d_key = jnp.einsum("sqk,sqd->skd", d_scores, query, preferred_element_type=F32)
    d_value = jnp.einsum("sqk,sqd->skd", probs_low, d_heads, preferred_element_type=F32)
    d_key = d_key.reshape(C, y_count, group_rows, HD)
    d_value = d_value.reshape(C, y_count, group_rows, HD)

    def kv_share(stream):
        return jnp.concatenate([d_key[stream], d_value[stream]], axis=-1).reshape(-1, 2 * HD)

    kv_share_own, kv_share_other = kv_share(0), kv_share(1).astype(BF)
    (
        kv_share_own, kv_share_other, d_query, gu_arrived, gu_last, d_proj_halves, heads_low, down_got
    ) = stage(
        kv_share_own, kv_share_other, d_query, gu_arrived, gu_cores[1], d_proj_halves, heads_low,
        down_got,
    )

    kv_sum = kv_share_own + swap_core(kv_share_other).astype(F32)
    kv_sum = kv_sum.reshape(y_count, group_rows, 2 * HD)
    own_kv = kv_sum[0]
    for k in range(1, y_count):
        own_kv = own_kv + give_to(kv_sum[k].astype(BF), "y", y_count, k).astype(F32)
    gu_next = z_send(lambda k: z_block(gu_last[:, :ff_own], k, shard))
    _, rot_pull = jax.vjp(rotated, q_raw, qk[0])
    d_q_raw, d_gain_query = rot_pull(d_query.reshape(C * group_rows, HD))
    _, rot_pull = jax.vjp(rotated_own, k_raw[:group_rows], qk[1])
    d_k_raw, d_gain_key = rot_pull(own_kv[:, :HD])
    _, unit_pull = jax.vjp(unit_norm, v_raw[:group_rows])
    (d_v_raw,) = unit_pull(own_kv[:, HD:])
    d_q_low = d_q_raw.astype(BF)
    d_kv_low = jnp.concatenate([d_k_raw.astype(BF), d_v_raw.astype(BF)], axis=-1)
    d_own_low = jnp.concatenate([d_q_low[:group_rows], d_kv_low], axis=-1)
    d_q_low, d_kv_low, d_own_low, gu_next, gu_last, down_grads, d_proj_halves = stage(
        d_q_low, d_kv_low, d_own_low, gu_next, gu_last[:, ff_own:], down_grads, d_proj_halves
    )

    part_other = times_t(d_q_low[group_rows:], qkv_mat[:, :HD])
    part_own = times_t(d_own_low, qkv_mat)
    gu_final = z_send(lambda k: z_block(gu_last, k, shard))
    blocks = core_sum(part_own, part_other)
    blocks, part_own, part_other, d_q_low, d_kv_low, normed_pieces, left_grads, gu_final = stage(
        blocks, part_own, part_other, d_q_low, d_kv_low, normed_pieces, left_grads, gu_final
    )
    gu_arrived = list(gu_arrived[0]) + list(gu_next) + list(gu_final)
    share_mid = give_to(blocks[2], "z", Z, 2)
    d_gain_input = (
        jnp.sum(part_own * unit_own, axis=0)
        + jnp.sum(part_other * unit_other, axis=0)
        + jnp.sum(d_normed_own * unit_norm(token_vals), axis=0)
    )
    d_qk = jnp.stack([d_gain_query, d_gain_key]).reshape(2, -1, qk_shard)
    d_qk = jnp.pad(d_qk, ((0, 0), (0, 0), (0, shard - qk_shard))).reshape(2, -1)
    gain_grads = jnp.stack(
        [d_gain_input, d_gain_post_attn, d_gain_laurel, d_gain_pre_ff, d_gain_post_ff, d_gain_ple]
    )
    gain_grads = jnp.concatenate([gain_grads, d_qk], axis=0)
    gain_grads = jnp.pad(gain_grads, ((0, 16 - gain_count - 2), (0, 0))).astype(BF)
    row_grads = jnp.concatenate([left_grads, gain_grads], axis=0)
    row_count = row_grads.shape[0]
    last_grads = []
    for p in range(yx):
        query_part = both_rows(normed_pieces[p], (d_q_low[:group_rows], d_q_low[group_rows:]))
        kv_part = over_rows(normed_pieces[p][0], d_kv_low).astype(BF)
        last_grads.append((query_part, kv_part))
    copies = []
    for p in range(yx):
        copies.append((C * p, 0, 0, p, 0, 0, tall, HD))
        copies.append((C * p + 1, 0, 0, p, 0, HD, tall, 2 * HD))
        for z in range(Z):
            column = (z * yx + places_yx[p], unit)
            copies.append((C * yx, 0, column, p, tall, z * unit, row_count, unit))
        copies.append((C * yx + 1, 0, 0, p, tall, tall, row_count, span - tall))
    last_grads = shuffle(
        [part for pair in last_grads for part in pair]
        + [row_grads, jnp.zeros((row_count, span - tall), BF)],
        [(tall + row_count, span)] * yx,
        copies,
    )
    share_mid, last_grads, blocks, heads_low, d_proj_halves, down_got, down_grads = stage(
        share_mid, last_grads, blocks, heads_low, d_proj_halves, down_got, down_grads
    )
    share_next = give_to(blocks[1], "z", Z, 1)
    last_got = sum_first(last_grads, y_count)
    out_grad = both_rows((heads_low[:group_rows], heads_low[group_rows:]), d_proj_halves)
    share_next, last_got, last_grads, out_grad, blocks, down_got, down_grads = stage(
        share_next, last_got, last_grads, out_grad, blocks, down_got, down_grads
    )
    shares = [blocks[0], share_mid, share_next, give_to(blocks[3], "z", Z, 3)]
    last_got = sum_second(last_grads, list(last_got), y_count)
    out_both = order_cores(*by_core(out_grad, yx // 2), first, 0)
    grad_down = sum_total(down_grads, down_got)
    shares, last_got, last_grads, out_both, gu_arrived, ple_arrived = stage(
        shares, last_got, last_grads, out_both, gu_arrived, ple_arrived
    )
    d_normed = d_normed_own + add_up(shares)

    last_low = sum_total(last_grads, last_got).astype(BF)
    qkv_pair = by_core(last_low[:tall], Z)
    qkv_cores = [jnp.where(first, *qkv_pair), jnp.where(first, *qkv_pair[::-1])]
    heights = [min(shard, row_count - low) for low in range(0, row_count, shard)]
    copies = []
    for k in range(Z):
        z_to = (zi + k) % Z
        for c in range(C):
            copies.append((c, (z_to, shard), 0, k, 0, c * span, shard, span))
        for j, height in enumerate(heights):
            copies.append(
                (2, tall + j * shard, (z_to, unit), k, 0, C * span + j * unit, height, unit)
            )
    last_sends = shuffle(
        qkv_cores + [last_low], [(shard, C * span + len(heights) * unit)] * Z, copies
    )
    last_sends, out_both, gu_arrived, ple_arrived, d_normed = stage(
        last_sends, out_both, gu_arrived, ple_arrived, d_normed
    )
    last_arrived = z_send(lambda k: last_sends[k])
    out_grads = [
        lax.dynamic_slice_in_dim(out_both, places_yx[p] * shard, shard) for p in range(yx)
    ]
    grad_out = sum_total(out_grads, sum_second(out_grads, sum_first(out_grads, y_count), y_count))
    ple_total = own_core(sum(piece.astype(F32) for piece in ple_arrived))
    _, norm_pull = jax.vjp(rms_norm, token_vals, gains[0])
    d_tokens_norm, _ = norm_pull(d_normed)
    d_tokens = d_branch + d_tokens_norm
    copies = []
    for k in range(Z):
        for c in range(C):
            for m in range(2):
                for a in range(yx):
                    column = (((zi - k) % Z * yx + a) * C + c, ff_shard)
                    source = (k, m * ff_own) if c == 0 else ((1 + m) * Z + k, 0)
                    copies.append(
                        (
                            source[0], 0, source[1] + a * ff_shard,
                            m, 0, column, shard, ff_shard,
                        )
                    )
    grad_gu = shuffle(list(gu_arrived), [(shard, Z * yx * C * ff_shard)] * 2, copies)
    grad_gu = [grad.astype(F32) for grad in grad_gu]
    qkv_parts = z_place(last_arrived, zi)[:, : C * span].astype(F32)
    row_total = sum(piece[:, C * span :].astype(F32) for piece in last_arrived)
    row_total = jnp.concatenate(
        [row_total[:height, j * unit : (j + 1) * unit] for j, height in enumerate(heights)], axis=0
    )
    row_keep = jnp.where(first, row_total[:, :shard], row_total[:, shard:])
    row_send = jnp.where(first, row_total[:, shard:], row_total[:, :shard])
    row_total = row_keep + swap_core(row_send.astype(BF)).astype(F32)

    def qkv_part(z, c, m):
        return qkv_parts[z * shard : (z + 1) * shard, (3 * c + m) * HD : (3 * c + m + 1) * HD]

    grad_query = jnp.concatenate([qkv_part(z, c, 0) for z in range(Z) for c in range(C)], axis=1)
    grad_kv = [
        jnp.concatenate(
            [
                sum(
                    qkv_part(z, c, m)
                    for z in range(h * Z // KVH, (h + 1) * Z // KVH)
                    for c in range(C)
                )
                for h in range(KVH)
            ],
            axis=1,
        )
        for m in (1, 2)
    ]
    grad_gains = row_total[lanes : lanes + gain_count]
    grad_qk = row_total[lanes + gain_count : lanes + gain_count + 2, :qk_shard]
    return (
        output.astype(BF)[None],
        d_tokens.astype(BF)[None],
        d_extra.astype(BF)[None],
        grad_query,
        grad_kv[0],
        grad_kv[1],
        grad_out,
        row_total[:left_rank].T,
        row_total[left_rank:lanes],
        grad_gains,
        grad_qk,
        grad_gu[0],
        grad_gu[1],
        grad_down,
        ple_total[:, :ple],
        ple_total[:, ple:].T,
    )


def solution(mesh):
    fine = Mesh(mesh.devices.reshape(Z, -1, X, C), EVERY)
    rows = P(EVERY, None)
    cols = P(None, EVERY)
    stream = P(("x", "c"), ("z", "y"), None)
    return jax.shard_map(
        local,
        mesh=fine,
        in_specs=(
            stream, stream, stream, P(("x", "c"), None), P(),
            rows, rows, rows, rows, rows, cols, cols, cols, rows, rows, rows, rows, cols,
        ),
        out_specs=(
            stream, stream, stream,
            rows, rows, rows, rows, rows, cols, cols, cols, rows, rows, rows, rows, cols,
        ),
        check_vma=False,
    )
```

```python
import jax
import jax.numpy as jnp
from jax import lax
from jax.experimental import pallas as pl
from jax.experimental.pallas import tpu as pltpu
from jax.sharding import Mesh, PartitionSpec as P

H = 8
KVH = 2
HD = 256
Z = 4
X = 2
C = 2

EPSILON = 1e-06
ROPE_BASE = 1000000.0
HALF_ROOT = 0.7071067811865476
MASKED = -1e30
BF = jnp.bfloat16
F32 = jnp.float32
EVERY = ("z", "y", "x", "c")


def rms_norm(values_in, gain_in):
    return (
        values_in
        * lax.rsqrt(jnp.mean(values_in * values_in, axis=-1, keepdims=True) + EPSILON)
        * gain_in
    )


def unit_norm(values_in):
    return values_in * lax.rsqrt(
        jnp.mean(values_in * values_in, axis=-1, keepdims=True) + EPSILON
    )


def gelu_tanh(values_in):
    return jax.nn.gelu(values_in, approximate=True)


def glu_piece(gate_in, up_in):
    return gelu_tanh(gate_in) * up_in


def rotate(values_in, cos_tab, sine_tab):
    half_width = values_in.shape[-1] // 2
    first_half = values_in[..., :half_width]
    second_half = values_in[..., half_width:]
    return jnp.concatenate(
        [
            first_half * cos_tab - second_half * sine_tab,
            second_half * cos_tab + first_half * sine_tab,
        ],
        axis=-1,
    )


def times(left_in, right_in):
    return jnp.einsum("...a,ab->...b", left_in, right_in, preferred_element_type=F32)


def times_t(left_in, right_in):
    return jnp.einsum("...a,ba->...b", left_in, right_in, preferred_element_type=F32)


def over_rows(left_in, right_in):
    return jnp.einsum("ra,rb->ab", left_in, right_in, preferred_element_type=F32)


def give_to(value, axis, size, step):
    return lax.ppermute(value, axis, [(i, (i + step) % size) for i in range(size)])


def swap_core(value):
    return lax.ppermute(value, "c", [(0, 1), (1, 0)])


def after(value, *others):
    return lax.optimization_barrier((value, *others))[0]


def pick(value, index, axis):
    return lax.dynamic_index_in_dim(value, index, axis, keepdims=False)


def stage(*values):
    return lax.optimization_barrier(values)


def start_of(spec):
    return spec[0] * spec[1] if isinstance(spec, tuple) else spec


def shuffle(arrays, outs, copies):
    dtype = arrays[0].dtype
    aligned = True
    for _, r_in, c_in, _, r_out, c_out, height, wide in copies:
        for spec, tile in ((r_in, 16), (r_out, 16), (c_in, 128), (c_out, 128)):
            size = spec[1] if isinstance(spec, tuple) else spec
            aligned = aligned and size % tile == 0
        aligned = aligned and height % 16 == 0 and wide % 128 == 0
    if not aligned:
        made = [jnp.zeros(shape, dtype) for shape in outs]
        for a, r_in, c_in, o, r_out, c_out, height, wide in copies:
            piece = lax.dynamic_slice(
                arrays[a], (start_of(r_in), start_of(c_in)), (height, wide)
            )
            made[o] = lax.dynamic_update_slice(made[o], piece, (start_of(r_out), start_of(c_out)))
        return made
    numbers = []

    def known(spec):
        if not isinstance(spec, tuple):
            return spec
        numbers.append(spec[0])
        return (len(numbers) - 1, spec[1])

    plan = [
        (a, known(r_in), known(c_in), o, known(r_out), known(c_out), height, wide)
        for a, r_in, c_in, o, r_out, c_out, height, wide in copies
    ]
    table = jnp.stack([jnp.asarray(n, jnp.int32) for n in numbers] or [jnp.int32(0)])
    count = len(arrays)

    def kernel(table_ref, *refs):
        ins, made = refs[:count], refs[count:]

        def at(spec):
            if isinstance(spec, tuple):
                return pl.multiple_of(table_ref[spec[0]] * spec[1], spec[1])
            return spec

        for a, r_in, c_in, o, r_out, c_out, height, wide in plan:
            from_row, from_column, to_row, to_column = at(r_in), at(c_in), at(r_out), at(c_out)
            step = 16
            while height % (2 * step) == 0 and 2 * step * wide <= 65536:
                step *= 2
            chunks = height // step

            def move(low):
                made[o][pl.ds(to_row + low, step), pl.ds(to_column, wide)] = ins[a][
                    pl.ds(from_row + low, step), pl.ds(from_column, wide)
                ]

            if chunks % 4 or chunks <= 8:
                for i in range(chunks):
                    move(i * step)
            else:

                @pl.loop(0, chunks // 4)
                def _(i):
                    for j in range(4):
                        move(pl.multiple_of(i * 4 * step, step) + j * step)

    moved = sum(height * wide for *_, height, wide in plan) * dtype.itemsize
    return pl.pallas_call(
        kernel,
        out_shape=[jax.ShapeDtypeStruct(shape, dtype) for shape in outs],
        grid_spec=pltpu.PrefetchScalarGridSpec(
            num_scalar_prefetch=1,
            grid=(1,),
            in_specs=[pl.BlockSpec(memory_space=pltpu.VMEM)] * count,
            out_specs=[pl.BlockSpec(memory_space=pltpu.VMEM)] * len(outs),
        ),
        cost_estimate=pl.CostEstimate(flops=0, bytes_accessed=2 * moved, transcendentals=0),
    )(table, *arrays)


def stack_rows(pieces):
    if len(pieces) == 1:
        return pieces[0]
    copies = []
    low = 0
    for i, piece in enumerate(pieces):
        copies.append((i, 0, 0, 0, low, 0, *piece.shape))
        low += piece.shape[0]
    return shuffle(pieces, [(low, pieces[0].shape[1])], copies)[0]


def z_take(block):
    taken = {k: give_to(block, "z", Z, -k) for k in (2, 3, 1)}
    return [block] + [taken[k] for k in range(1, Z)]


def flat_step(step_y, step_x, y_count):
    return [
        (y * X + x, ((y + step_y) % y_count) * X + (x + step_x) % X)
        for y in range(y_count)
        for x in range(X)
    ]


def all_steps(y_count):
    return [(p // X, p % X) for p in range(1, y_count * X)]


def gather_first(block, y_count):
    if y_count == 2:
        return [give_to(block, "x", X, 1), give_to(block, "y", 2, 1)]
    return [
        lax.ppermute(block, ("y", "x"), flat_step(-dy, -dx, y_count)) for dy, dx in all_steps(y_count)
    ]


def gather_second(block, got, y_count):
    if y_count == 2:
        half = block.shape[0] // 2
        return got + [give_to(got[0][:half], "y", 2, 1), give_to(got[1][half:], "x", X, 1)]
    return got


def gather_parts(block, got, y_count):
    arrays = [block] + list(got)
    rows = block.shape[0]
    parts = [[(i, 0, rows)] for i in range(len(arrays))]
    if y_count == 2:
        parts = parts[:3] + [[(3, 0, rows // 2), (4, 0, rows // 2)]]
    return arrays, parts


def sum_first(pieces, y_count):
    if y_count == 2:
        half = pieces[3].shape[0] // 2
        return [give_to(pieces[3][:half], "x", X, 1), give_to(pieces[3][half:], "y", 2, 1)]
    return [
        lax.ppermute(pieces[dy * X + dx], ("y", "x"), flat_step(dy, dx, y_count))
        for dy, dx in all_steps(y_count)
    ]


def add_low(first_in, second_in):
    return (first_in.astype(F32) + second_in.astype(F32)).astype(BF)


def sum_second(pieces, got, y_count):
    if y_count == 2:
        half = pieces[3].shape[0] // 2
        to_y = jnp.concatenate([add_low(pieces[2][:half], got[0]), pieces[2][half:]], axis=0)
        to_x = jnp.concatenate([pieces[1][:half], add_low(pieces[1][half:], got[1])], axis=0)
        return [give_to(to_y, "y", 2, 1), give_to(to_x, "x", X, 1)]
    return got


def sum_total(pieces, got):
    return add_up([pieces[0]] + list(got))


def core_sum(own, other):
    total = own + swap_core(other.astype(BF)).astype(F32)
    rows = total.shape[0] // Z
    return [total[:rows]] + [
        total[k * rows : (k + 1) * rows].astype(BF) for k in range(1, Z)
    ]


def z_shares(blocks):
    given = {k: give_to(blocks[k], "z", Z, k) for k in (2, 3, 1)}
    return [blocks[0]] + [given[k] for k in range(1, Z)]


def add_up(pieces):
    total = pieces[0].astype(F32)
    for piece in pieces[1:]:
        total = total + piece.astype(F32)
    return total


def write_rows(pieces, starts):
    rows, width = pieces[0].shape
    whole = jnp.zeros((rows * len(pieces), width), pieces[0].dtype)
    for piece, start in zip(pieces, starts):
        whole = lax.dynamic_update_slice_in_dim(whole, piece, start, 0)
    return whole


def z_send(sends):
    given = {k: give_to(sends(k), "z", Z, k) for k in (2, 3, 1)}
    return [sends(0)] + [given[k] for k in range(1, Z)]


def z_place(arrived, zi):
    rows, width = arrived[0].shape
    copies = [(k, 0, 0, 0, ((zi - k) % Z, rows), 0, rows, width) for k in range(Z)]
    return shuffle(arrived, [(Z * rows, width)], copies)[0]


def order_cores(own, other, first, axis):
    return jnp.concatenate(
        [jnp.where(first, own, other), jnp.where(first, other, own)], axis=axis
    )


def places(pair_of, lengths, ctx_ids, row_count):
    blocks_last = 2 * pair_of.shape[0] - 1
    half_rows = row_count // 2
    pair = pair_of[ctx_ids][:, None]
    row = jnp.arange(row_count, dtype=jnp.int32)[None, :]
    block = jnp.where(row < half_rows, pair, blocks_last - pair)
    position = (block * half_rows + row % half_rows).reshape(-1)
    ends = jnp.cumsum(lengths, dtype=jnp.int32)
    before = ends[None, :] <= position[:, None]
    segment = jnp.sum(before.astype(jnp.int32), axis=1, dtype=jnp.int32)
    start = jnp.sum(jnp.where(before, lengths[None, :], 0), axis=1, dtype=jnp.int32)
    return position, segment, position - start


def local(
    tokens,
    layer_input,
    cotangent,
    doc_lengths,
    pair_of,
    w_query,
    w_key,
    w_value,
    w_out,
    w_left,
    w_right,
    norm_gains,
    qk_gain,
    w_gate,
    w_up,
    w_down,
    w_pgate,
    w_pproj,
):
    rows = tokens.shape[1]
    width = tokens.shape[2]
    y_count = lax.axis_size("y")
    zi, yi, xi, ci = (lax.axis_index(name) for name in EVERY)
    first = ci == 0
    shard = w_query.shape[0]
    ff_shard = w_down.shape[0]
    yx = y_count * X
    unit = C * shard
    places_yx = [((yi + p // X) % y_count) * X + (xi + p % X) % X for p in range(yx)]
    tall = Z * unit

    def place_parts(block, got, cuts):
        arrays, parts = gather_parts(block, got, y_count)
        copies = []
        for p in range(yx):
            z = 0
            for i, _, height in parts[p]:
                for low in range(0, height, unit):
                    to = (z * yx + places_yx[p], unit)
                    for o, (left_edge, right_edge) in enumerate(cuts):
                        copies.append(
                            (i, low, left_edge, o, to, 0, unit, right_edge - left_edge)
                        )
                    z += 1
        outs = [(Z * yx * unit, high - low) for low, high in cuts]
        return shuffle(arrays, outs, copies)

    def place_blocks(block, got, height):
        arrays, parts = gather_parts(block, got, y_count)
        copies = []
        for p in range(yx):
            low = 0
            for i, _, part in parts[p]:
                to = (places_yx[p] * (height // part) + low // part, part)
                copies.append((i, 0, 0, 0, to, 0, part, block.shape[1]))
                low += part
        return shuffle(arrays, [(yx * height, block.shape[1])], copies)[0]

    def row_pieces(value):
        value = value.reshape(Z, yx, unit, -1)
        return [pick(value, places_yx[p], 1).reshape(tall, -1) for p in range(yx)]

    def column_pieces(halves):
        copies = []
        for p in range(yx):
            for h in range(C):
                for z in range(Z):
                    column = (z * yx + places_yx[p], unit)
                    copies.append(
                        (h, 0, column, p * C + h, 0, z * unit, halves[h].shape[0], unit)
                    )
        made = shuffle(list(halves), [(halves[0].shape[0], tall)] * (C * yx), copies)
        return [made[p * C : p * C + C] for p in range(yx)]

    def pair_cores(own, height):
        other = swap_core(own)
        last = own.shape[1]
        cores = [jnp.where(first, own, other), jnp.where(first, other, own)]
        return jnp.concatenate([core.reshape(-1, 1, height, last) for core in cores], axis=1)

    left_rank = w_left.shape[1]
    ple = w_pgate.shape[1]
    gain_count = norm_gains.shape[0]
    qk_shard = qk_gain.shape[1]
    ff_own = yx * ff_shard
    lanes = 2 * left_rank
    span = 3 * HD

    group_rows = Z * rows

    def z_block(value, k, height, axis=0):
        return lax.dynamic_slice_in_dim(value, (zi + k) % Z * height, height, axis=axis)

    gain_pack = jnp.concatenate(
        [
            jnp.pad(norm_gains, ((0, 0), (0, lanes - shard))),
            jnp.pad(qk_gain, ((0, 0), (0, lanes - qk_shard))),
        ],
        axis=0,
    )
    gain_rows = gain_count + 2
    qkv_low = jnp.concatenate(
        [w_query, w_key, w_value, jnp.pad(gain_pack, ((0, shard - gain_rows), (0, 0)))], axis=1
    ).astype(BF)
    qkv_got = swap_core(qkv_low)
    qkv_low, qkv_got, out_late = stage(qkv_low, qkv_got, w_out)

    gain_low = (H + 2 * KVH) * HD
    own_gain, other_gain = qkv_low[:gain_rows, gain_low:], qkv_got[:gain_rows, gain_low:]
    gain_block = jnp.concatenate(
        [
            jnp.where(first, own_gain, other_gain),
            jnp.where(first, other_gain, own_gain),
            jnp.zeros((max(shard - C * gain_rows, 0), lanes), BF),
        ],
        axis=0,
    )[:shard]
    misc = jnp.concatenate(
        [
            jnp.concatenate([w_left, w_right.T, w_pgate], axis=1).astype(BF),
            jnp.concatenate([gain_block, w_pproj.T.astype(BF)], axis=1),
        ],
        axis=0,
    )
    copies = []
    for k in range(Z):
        z_to = (zi + k) % Z
        head = z_to * KVH // Z
        columns = [z_to * C + ci, H + head, H + KVH + head]
        for a, c_from in ((0, ci), (1, 1 - ci)):
            for j, column in enumerate(columns):
                copies.append((a, 0, (column, HD), k, (c_from, shard), j * HD, shard, HD))
        copies.append((2, 0, 0, k, 0, span, unit, misc.shape[1]))
    first_sends = shuffle(
        [qkv_low, qkv_got, misc], [(unit, span + misc.shape[1])] * Z, copies
    )
    first_arrived = z_send(lambda k: first_sends[k])
    gate_late, up_late, out_late, _ = stage(w_gate, w_up, out_late, first_sends)
    ff_low = jnp.concatenate([gate_late, up_late], axis=1).astype(BF)
    ff_got = swap_core(ff_low)
    out_low = out_late.astype(BF)
    out_x = give_to(out_low, "x", X, 1) if y_count == 2 else out_low
    own_tokens, pair_of, first_arrived, ff_low, ff_got, out_low, out_x = stage(
        tokens[0], pair_of, first_arrived, ff_low, ff_got, out_low, out_x
    )

    token_take = z_take(own_tokens)
    first_rows = z_place(first_arrived, zi)
    first_got = gather_first(first_rows, y_count)
    copies = []
    for m in range(2):
        for k in range(Z):
            for a in range(yx):
                part, low = divmod(a, yx // 2)
                for source, c_from in ((0, ci), (1, 1 - ci)):
                    column = (((m * Z + (zi + k) % Z) * yx + a) * C + ci, ff_shard)
                    copies.append(
                        (
                            source, 0, column, (2 * m + part) * Z + k, (c_from, shard),
                            low * ff_shard, shard, ff_shard,
                        )
                    )
    ff_sends = shuffle([ff_low, ff_got], [(unit, ff_own // 2)] * (4 * Z), copies)
    ff_sends = [ff_sends[j * Z : (j + 1) * Z] for j in range(4)]
    out_pair = stack_rows([out_low, out_x])
    first_rows, first_got = stage(first_rows, first_got)
    first_got = gather_second(first_rows, list(first_got), y_count)

    lengths = [doc_lengths[0], swap_core(doc_lengths)[0]]
    z_ids = (zi + jnp.arange(Z)) % Z
    own_ids = z_ids * y_count + yi
    key_ids = (z_ids[None, :] * y_count + ((yi + jnp.arange(y_count)) % y_count)[:, None]).reshape(-1)
    visible = []
    relative = []
    for lens in lengths:
        q_pos, q_seg, q_rel = places(pair_of, lens, own_ids, rows)
        k_pos, k_seg, _ = places(pair_of, lens, key_ids, rows)
        seen = (k_seg[None, :] == q_seg[:, None]) & (k_pos[None, :] <= q_pos[:, None])
        visible.append(seen.astype(F32))
        relative.append(q_rel)
    visible = jnp.stack(visible)
    relative = jnp.concatenate(relative)
    frequency = ROPE_BASE ** (-2.0 * jnp.arange(HD // 2, dtype=F32) / HD)
    angles = relative.astype(F32)[:, None] * frequency[None, :]
    cos_tab, sine_tab = jnp.cos(angles), jnp.sin(angles)
    qkv_mat, misc_all, small_late = place_parts(
        first_rows,
        first_got,
        [(0, span), (span, span + lanes), (span + lanes, span + lanes + ple)],
    )
    gain_all = misc_all.reshape(-1, unit, lanes)[:, shard : shard + C * gain_rows, :shard]
    gain_all = gain_all.reshape(-1, gain_rows, shard).transpose(1, 0, 2)
    gains = gain_all[:gain_count].reshape(gain_count, -1).astype(F32)
    qk = gain_all[gain_count:, :, :qk_shard].reshape(2, -1).astype(F32)
    (
        token_take, qkv_mat, misc_all, small_late, gains, qk, ff_sends, visible, cos_tab, sine_tab,
        out_pair,
    ) = stage(
        token_take, qkv_mat, misc_all, small_late, gains, qk, ff_sends, visible, cos_tab, sine_tab,
        out_pair,
    )
    visible = visible > 0.5

    def rotated(raw_in, gain_in):
        return rotate(rms_norm(raw_in, gain_in), cos_tab, sine_tab)

    def rotated_own(raw_in, gain_in):
        return rotate(rms_norm(raw_in, gain_in), cos_tab[:group_rows], sine_tab[:group_rows])

    token_own = stack_rows(token_take)
    token_other = swap_core(token_own)
    ff_arrived = [z_send(lambda k: ff_sends[0][k])]
    lr_own = misc_all.reshape(-1, unit, lanes)[:, :shard].reshape(-1, lanes)
    unit_own = unit_norm(token_own.astype(F32))
    unit_other = unit_norm(token_other.astype(F32))
    normed_own = (unit_own * gains[0]).astype(BF)
    normed_other = (unit_other * gains[0]).astype(BF)
    qkv = jnp.concatenate([times(normed_own, qkv_mat), times(normed_other, qkv_mat)], axis=0)
    q_raw, k_raw, v_raw = qkv[:, :HD], qkv[:, HD : 2 * HD], qkv[:, 2 * HD :]
    query = rotated(q_raw, qk[0]).astype(BF).reshape(C, group_rows, HD)
    key = rotated(k_raw, qk[1]).astype(BF)
    value = unit_norm(v_raw).astype(BF)
    kv = jnp.concatenate([key, value], axis=-1).reshape(C, group_rows, 2 * HD)
    out_y = give_to(out_pair, "y", 2, 1) if y_count == 2 else out_pair
    kv, query, ff_arrived, ff_sends, out_pair, out_y, lr_own, small_own = stage(
        kv, query, ff_arrived, ff_sends, out_pair, out_y, lr_own, small_late
    )
    ff_arrived = list(ff_arrived) + [z_send(lambda k: ff_sends[1][k])]

    kv_own = [kv[0]] + [give_to(kv[0], "y", y_count, -k) for k in range(1, y_count)]
    if y_count == 2:
        copies = []
        for p in range(yx):
            copies.append(
                (p // X, p % X * shard, 0, 0, (places_yx[p], shard), 0, shard, width)
            )
        out_rows = shuffle([out_pair, out_y], [(yx * shard, width)], copies)[0]
        out_half = yx // 2 * shard
        out_got = swap_core(lax.dynamic_slice_in_dim(out_rows, (1 - ci) * out_half, out_half))
    else:
        out_rows = lax.all_gather(out_pair[:shard], ("y", "x", "c"), axis=0, tiled=True)
        out_got = out_rows
    kv_own, ff_arrived, ff_sends, out_rows, out_got = stage(
        kv_own, ff_arrived, ff_sends, out_rows, out_got
    )

    if y_count == 2:
        copies = []
        for a in range(yx // 2):
            copies.append(
                (0, (ci * (yx // 2) + a, shard), 0, 0, (a * C + ci, shard), 0, shard, width)
            )
            copies.append((1, a * shard, 0, 0, (a * C + 1 - ci, shard), 0, shard, width))
        out_mat = shuffle([out_rows, out_got], [(HD, width)], copies)[0]
    else:
        out_mat = lax.dynamic_slice_in_dim(out_rows, ci * HD, HD)
    ff_arrived = list(ff_arrived) + [z_send(lambda k: ff_sends[2][k])]
    kv_other = [kv[1]] + [swap_core(piece) for piece in kv_own[1:]]
    kv_all = jnp.stack([jnp.concatenate(kv_own), jnp.concatenate(kv_other)])
    key_all, value_all = kv_all[..., :HD], kv_all[..., HD:]
    scores = jnp.einsum("sqd,skd->sqk", query, key_all, preferred_element_type=F32)
    scores = jnp.where(visible, scores, MASKED)
    top = jnp.max(scores, axis=-1, keepdims=True)
    log_total = top + jnp.log(jnp.sum(jnp.exp(scores - top), axis=-1, keepdims=True))
    probs = jnp.exp(scores - log_total)
    probs_low = probs.astype(BF)
    head_out = jnp.einsum("sqk,skd->sqd", probs_low, value_all, preferred_element_type=F32)
    heads_low = head_out.astype(BF).reshape(C * group_rows, HD)
    heads_low, ff_arrived, ff_sends, out_mat, lr_own = stage(
        heads_low, ff_arrived, ff_sends, out_mat, lr_own
    )

    heads_share = times(heads_low[group_rows:], out_mat)
    ff_arrived = list(ff_arrived) + [z_send(lambda k: ff_sends[3][k])]
    lr_other = swap_core(lr_own)
    blocks = core_sum(times(heads_low[:group_rows], out_mat), heads_share)
    blocks, ff_arrived, lr_own, lr_other, own_tokens, heads_low = stage(
        blocks, ff_arrived, lr_own, lr_other, own_tokens, heads_low
    )
    copies = [
        (j * Z + k, 0, 0, 0, ((zi - k) % Z, unit), j * (ff_own // 2), unit, ff_own // 2)
        for j in range(4)
        for k in range(Z)
    ]
    gu_rows = shuffle(
        [piece for pieces in ff_arrived for piece in pieces], [(tall, 2 * ff_own)], copies
    )[0]
    shares = z_shares(blocks)
    gu_got = gather_first(gu_rows, y_count)

    def core_rows(own, other):
        last = own.shape[1]
        cores = [jnp.where(first, own, other), jnp.where(first, other, own)]
        return jnp.concatenate(
            [core.reshape(-1, 1, shard, last) for core in cores], axis=1
        ).reshape(-1, last)

    lr_mat = core_rows(lr_own, lr_other)
    left_mat, right_mat = lr_mat[:, :left_rank], lr_mat[:, left_rank:]
    token_vals = own_tokens.astype(F32)
    normed = rms_norm(token_vals, gains[0])
    normed_low = normed.astype(BF)
    left_low = times(normed_low, left_mat).astype(BF)
    right_out = times_t(left_low, right_mat)
    laurel = normed + rms_norm(right_out, gains[2])
    shares, gu_rows, gu_got, laurel, w_down = stage(shares, gu_rows, gu_got, laurel, w_down)

    projected = add_up(shares)
    gated_sum = token_vals + rms_norm(projected, gains[1])
    joined = (gated_sum + laurel) * HALF_ROOT
    ff_in = rms_norm(joined, gains[3]).astype(BF)
    ff_in, gu_got, gu_rows, w_down = stage(ff_in, gu_got, gu_rows, w_down)
    ff_take = z_take(ff_in)
    down_low = w_down.astype(BF)
    if y_count == 2:
        half = tall // 2
        pass_y = shuffle(
            [gu_got[0], down_low],
            [(half + down_low.shape[0], width)],
            [(0, 0, 0, 0, 0, 0, half, width), (1, 0, 0, 0, half, 0, *down_low.shape)],
        )[0]
        pass_x = shuffle(
            [gu_got[1], down_low],
            [(half + down_low.shape[0], width)],
            [(0, half, 0, 0, 0, 0, half, width), (1, 0, 0, 0, half, 0, *down_low.shape)],
        )[0]
        passed = [give_to(pass_y, "y", 2, 1), give_to(pass_x, "x", X, 1)]
    else:
        passed = gather_first(down_low, y_count)
    ff_take, gu_rows, gu_got, down_low, passed = stage(ff_take, gu_rows, gu_got, down_low, passed)

    ff_rows = stack_rows(ff_take)
    ff_halves = [ff_rows, swap_core(ff_rows)]
    if y_count == 2:
        edge = down_low.shape[0] // 2
        down_far = [
            give_to(passed[1][half : half + edge], "y", 2, 1),
            give_to(passed[0][half + edge :], "x", X, 1),
        ]
        copies = []
        sources = [[(0, 0)], [(1, 0)], [(2, 0)], [(3, 0), (4, 0)]]
        for p in range(yx):
            for z in range(Z):
                part, low = sources[p][0] if p < 3 else sources[p][z * 2 // Z]
                low = z * unit if p < 3 else (z * unit) % half
                copies.append(
                    (part, low, 0, 0, (z * yx + places_yx[p], unit), 0, unit, width)
                )
        gu_mat = shuffle(
            [gu_rows, gu_got[0], gu_got[1], passed[0], passed[1]], [(Z * yx * unit, width)], copies
        )[0]
    else:
        down_far = passed
        gu_mat = place_parts(gu_rows, gu_got, [(0, 2 * ff_own)])[0]
    gate_proj, up_proj, hidden = [], [], []
    for part in ff_halves:
        gate_up = times(part, gu_mat)
        gate_proj.append(gate_up[:, :ff_own])
        up_proj.append(gate_up[:, ff_own:])
        hidden.append(glu_piece(gate_proj[-1], up_proj[-1]).astype(BF))
    hidden, down_far, small_own = stage(hidden, down_far, small_own)

    if y_count == 2:
        copies = [
            (0, 0, 0, 0, (places_yx[0], ff_shard), 0, ff_shard, width),
            (2, half, 0, 0, (places_yx[1], ff_shard), 0, ff_shard, width),
            (1, half, 0, 0, (places_yx[2], ff_shard), 0, ff_shard, width),
            (3, 0, 0, 0, (places_yx[3] * 2, edge), 0, edge, width),
            (4, 0, 0, 0, (places_yx[3] * 2 + 1, edge), 0, edge, width),
        ]
        down_mat = shuffle(
            [down_low, passed[0], passed[1], down_far[0], down_far[1]],
            [(yx * ff_shard, width)],
            copies,
        )[0]
    else:
        down_mat = place_blocks(down_low, down_far, ff_shard)
    down_share = times(hidden[1], down_mat)
    small_other = swap_core(small_own)
    blocks = core_sum(times(hidden[0], down_mat), down_share)
    blocks, small_own, small_other = stage(blocks, small_own, small_other)
    shares = z_shares(blocks)

    def small_rows(value):
        value = value.reshape(-1, C, shard, ple)
        return jnp.concatenate([value[:, 0], value[:, 1]], axis=-1).reshape(-1, 2 * ple)

    ple_mat = core_rows(small_rows(small_own), small_rows(small_other))
    shares, ple_mat = stage(shares, ple_mat)
    pgate_mat, pproj_mat = ple_mat[:, :ple], ple_mat[:, ple:]
    down_proj = add_up(shares)

    extra_vals = layer_input[0].astype(F32)
    after_ff = joined + rms_norm(down_proj, gains[4])
    after_low = after_ff.astype(BF)
    per_gate = times(after_low, pgate_mat)
    per_mix = glu_piece(per_gate, extra_vals).astype(BF)
    per_out = times_t(per_mix, pproj_mat)
    d_output = cotangent[0].astype(F32)
    _, norm_pull = jax.vjp(rms_norm, per_out, gains[5])
    d_per_out, d_gain_ple = norm_pull(d_output)
    d_per_low = d_per_out.astype(BF)
    d_per_mix = times(d_per_low, pproj_mat)
    _, glu_pull = jax.vjp(glu_piece, per_gate, extra_vals)
    d_per_gate, d_extra = glu_pull(d_per_mix)
    d_pgate_low = d_per_gate.astype(BF)
    d_after = d_output + times_t(d_pgate_low, pgate_mat)
    _, norm_pull = jax.vjp(rms_norm, down_proj, gains[4])
    d_down, d_gain_post_ff = norm_pull(d_after)
    d_down_low = d_down.astype(BF)
    (
        d_down_low, after_late, d_pgate_late, d_per_late, per_mix_late, after_ff, per_out, d_gain_ple,
        d_gain_post_ff, d_extra,
    ) = stage(
        d_down_low, after_low, d_pgate_low, d_per_low, per_mix, after_ff, per_out, d_gain_ple,
        d_gain_post_ff, d_extra,
    )

    d_down_take = z_take(d_down_low)
    output = after_ff + rms_norm(per_out, gains[5])
    ple_grads = row_pieces(
        jnp.concatenate(
            [over_rows(after_late, d_pgate_late), over_rows(d_per_late, per_mix_late)], axis=1
        ).astype(BF)
    )
    ple_got = sum_first(ple_grads, y_count)
    d_down_take, ple_grads, ple_got = stage(d_down_take, ple_grads, ple_got)

    d_down_rows = stack_rows(d_down_take)
    d_down_halves = [d_down_rows, swap_core(d_down_rows)]
    ple_got = sum_second(ple_grads, list(ple_got), y_count)
    d_gu_low = []
    for h in range(C):
        d_hidden = times_t(d_down_halves[h], down_mat)
        _, glu_pull = jax.vjp(glu_piece, gate_proj[h], up_proj[h])
        d_gate, d_up = glu_pull(d_hidden)
        d_gu_low.append(jnp.concatenate([d_gate.astype(BF), d_up.astype(BF)], axis=-1))
    d_gu_low, ple_got = stage(d_gu_low, ple_got)

    term_share = times_t(d_gu_low[1], gu_mat)
    ple_sum = sum_total(ple_grads, ple_got).astype(BF)
    ple_arrived = z_send(lambda k: z_block(ple_sum, k, unit))
    blocks = core_sum(times_t(d_gu_low[0], gu_mat), term_share)
    blocks, d_gu_low, ff_halves, hidden, d_down_halves, ple_arrived = stage(
        blocks, d_gu_low, ff_halves, hidden, d_down_halves, ple_arrived
    )
    share_mid = give_to(blocks[2], "z", Z, 2)

    def own_core(total):
        keep = jnp.where(first, total[:shard], total[shard:])
        send = jnp.where(first, total[shard:], total[:shard])
        return keep + swap_core(send.astype(BF)).astype(F32)

    def both_rows(lefts, rights):
        return (over_rows(lefts[0], rights[0]) + over_rows(lefts[1], rights[1])).astype(BF)

    gu_grads = [None] * yx
    down_grads = [None] * yx
    ff_pieces = column_pieces(ff_halves)

    def down_grad(p):
        return both_rows(
            [
                lax.dynamic_slice_in_dim(half_in, places_yx[p] * ff_shard, ff_shard, axis=1)
                for half_in in hidden
            ],
            d_down_halves,
        )

    gu_grads[yx - 1] = both_rows(ff_pieces[yx - 1], d_gu_low)
    down_grads[yx - 1] = down_grad(yx - 1)
    merged = [jnp.zeros((16, 128), BF)]
    if y_count == 2:
        merged = [
            shuffle(
                [gu_grads[3], down_grads[3]],
                [(half + edge, width)],
                [
                    (0, side * half, 0, 0, 0, 0, half, width),
                    (1, side * edge, 0, 0, half, 0, edge, width),
                ],
            )[0]
            for side in range(2)
        ]
    (
        share_mid, merged, blocks, ff_pieces, d_gu_low, hidden, d_down_halves, gu_grads[yx - 1],
        down_grads[yx - 1],
    ) = stage(
        share_mid, merged, blocks, ff_pieces, d_gu_low, hidden, d_down_halves, gu_grads[yx - 1],
        down_grads[yx - 1],
    )
    shares = [blocks[0], give_to(blocks[1], "z", Z, 1), give_to(blocks[3], "z", Z, 3), share_mid]
    if y_count == 2:
        merged_got = [give_to(merged[0], "x", X, 1), give_to(merged[1], "y", 2, 1)]
    for p in range(yx - 1):
        gu_grads[p] = both_rows(ff_pieces[p], d_gu_low)
        down_grads[p] = down_grad(p)
    if y_count != 2:
        merged_got = sum_first(gu_grads, y_count)
    shares, merged_got, gu_grads, down_grads = stage(shares, merged_got, gu_grads, down_grads)
    term = add_up(shares)
    if y_count == 2:
        gu_got = [got[:half] for got in merged_got]
        down_got = [got[half:] for got in merged_got]
    else:
        gu_got = list(merged_got)

    _, norm_pull = jax.vjp(rms_norm, joined, gains[3])
    d_joined_norm, d_gain_pre_ff = norm_pull(term)
    d_branch = (d_after + d_joined_norm) * HALF_ROOT
    _, norm_pull = jax.vjp(rms_norm, projected, gains[1])
    d_projected, d_gain_post_attn = norm_pull(d_branch)
    d_proj_low = d_projected.astype(BF)
    (
        d_proj_low, d_branch, d_gain_pre_ff, d_gain_post_attn, right_out, normed_own, normed_other
    ) = stage(
        d_proj_low, d_branch, d_gain_pre_ff, d_gain_post_attn, right_out, normed_own, normed_other
    )

    d_proj_take = z_take(d_proj_low)
    gu_got = sum_second(gu_grads, gu_got, y_count)
    _, norm_pull = jax.vjp(rms_norm, right_out, gains[2])
    d_right, d_gain_laurel = norm_pull(d_branch)
    d_right_low = d_right.astype(BF)
    d_left_low = times(d_right_low, right_mat).astype(BF)
    d_normed_own = d_branch + times_t(d_left_low, left_mat)
    left_grads = jnp.concatenate(
        [over_rows(d_left_low, normed_low), over_rows(left_low, d_right_low)], axis=0
    ).astype(BF)
    normed_pieces = column_pieces((normed_own, normed_other))
    d_proj_take, gu_got, left_grads, normed_pieces, d_normed_own = stage(
        d_proj_take, gu_got, left_grads, normed_pieces, d_normed_own
    )

    def by_core(rows_in, blocks):
        even = jnp.concatenate(
            [rows_in[2 * j * shard : (2 * j + 1) * shard] for j in range(blocks)], axis=0
        )
        odd = jnp.concatenate(
            [rows_in[(2 * j + 1) * shard : (2 * j + 2) * shard] for j in range(blocks)], axis=0
        )
        return jnp.where(first, even, odd), swap_core(jnp.where(first, odd, even))

    d_proj_rows = stack_rows(d_proj_take)
    d_proj_halves = [d_proj_rows, swap_core(d_proj_rows)]
    gu_sum = sum_total(gu_grads, gu_got).astype(BF)
    gu_pair = by_core(gu_sum, Z)
    gu_cores = [jnp.where(first, *gu_pair), jnp.where(first, *gu_pair[::-1])]
    d_heads = jnp.concatenate([times_t(half_in, out_mat) for half_in in d_proj_halves], axis=0)
    if y_count != 2:
        down_got = sum_first(down_grads, y_count)
    gu_arrived = [z_send(lambda k: z_block(gu_cores[0], k, shard))]
    down_got = sum_second(down_grads, down_got, y_count)
    d_heads = d_heads.astype(BF).reshape(C, group_rows, HD)
    delta = jnp.sum(d_heads.astype(F32) * head_out, axis=-1, keepdims=True)
    d_probs = jnp.einsum("sqd,skd->sqk", d_heads, value_all, preferred_element_type=F32)
    d_scores = (probs * (d_probs - delta)).astype(BF)
    d_query = jnp.einsum("sqk,skd->sqd", d_scores, key_all, preferred_element_type=F32)
    d_key = jnp.einsum("sqk,sqd->skd", d_scores, query, preferred_element_type=F32)
    d_value = jnp.einsum("sqk,sqd->skd", probs_low, d_heads, preferred_element_type=F32)
    d_key = d_key.reshape(C, y_count, group_rows, HD)
    d_value = d_value.reshape(C, y_count, group_rows, HD)

    def kv_share(stream):
        return jnp.concatenate([d_key[stream], d_value[stream]], axis=-1).reshape(-1, 2 * HD)

    kv_share_own, kv_share_other = kv_share(0), kv_share(1).astype(BF)
    (
        kv_share_own, kv_share_other, d_query, gu_arrived, gu_last, d_proj_halves, heads_low, down_got
    ) = stage(
        kv_share_own, kv_share_other, d_query, gu_arrived, gu_cores[1], d_proj_halves, heads_low,
        down_got,
    )

    kv_sum = kv_share_own + swap_core(kv_share_other).astype(F32)
    kv_sum = kv_sum.reshape(y_count, group_rows, 2 * HD)
    own_kv = kv_sum[0]
    for k in range(1, y_count):
        own_kv = own_kv + give_to(kv_sum[k].astype(BF), "y", y_count, k).astype(F32)
    gu_next = z_send(lambda k: z_block(gu_last[:, :ff_own], k, shard))
    _, rot_pull = jax.vjp(rotated, q_raw, qk[0])
    d_q_raw, d_gain_query = rot_pull(d_query.reshape(C * group_rows, HD))
    _, rot_pull = jax.vjp(rotated_own, k_raw[:group_rows], qk[1])
    d_k_raw, d_gain_key = rot_pull(own_kv[:, :HD])
    _, unit_pull = jax.vjp(unit_norm, v_raw[:group_rows])
    (d_v_raw,) = unit_pull(own_kv[:, HD:])
    d_q_low = d_q_raw.astype(BF)
    d_kv_low = jnp.concatenate([d_k_raw.astype(BF), d_v_raw.astype(BF)], axis=-1)
    d_own_low = jnp.concatenate([d_q_low[:group_rows], d_kv_low], axis=-1)
    d_q_low, d_kv_low, d_own_low, gu_next, gu_last, down_grads, d_proj_halves = stage(
        d_q_low, d_kv_low, d_own_low, gu_next, gu_last[:, ff_own:], down_grads, d_proj_halves
    )

    part_other = times_t(d_q_low[group_rows:], qkv_mat[:, :HD])
    part_own = times_t(d_own_low, qkv_mat)
    gu_final = z_send(lambda k: z_block(gu_last, k, shard))
    blocks = core_sum(part_own, part_other)
    blocks, part_own, part_other, d_q_low, d_kv_low, normed_pieces, left_grads, gu_final = stage(
        blocks, part_own, part_other, d_q_low, d_kv_low, normed_pieces, left_grads, gu_final
    )
    gu_arrived = list(gu_arrived[0]) + list(gu_next) + list(gu_final)
    share_mid = give_to(blocks[2], "z", Z, 2)
    d_gain_input = (
        jnp.sum(part_own * unit_own, axis=0)
        + jnp.sum(part_other * unit_other, axis=0)
        + jnp.sum(d_normed_own * unit_norm(token_vals), axis=0)
    )
    d_qk = jnp.stack([d_gain_query, d_gain_key]).reshape(2, -1, qk_shard)
    d_qk = jnp.pad(d_qk, ((0, 0), (0, 0), (0, shard - qk_shard))).reshape(2, -1)
    gain_grads = jnp.stack(
        [d_gain_input, d_gain_post_attn, d_gain_laurel, d_gain_pre_ff, d_gain_post_ff, d_gain_ple]
    )
    gain_grads = jnp.concatenate([gain_grads, d_qk], axis=0)
    gain_grads = jnp.pad(gain_grads, ((0, 16 - gain_count - 2), (0, 0))).astype(BF)
    row_grads = jnp.concatenate([left_grads, gain_grads], axis=0)
    row_count = row_grads.shape[0]
    last_grads = []
    for p in range(yx):
        query_part = both_rows(normed_pieces[p], (d_q_low[:group_rows], d_q_low[group_rows:]))
        kv_part = over_rows(normed_pieces[p][0], d_kv_low).astype(BF)
        last_grads.append((query_part, kv_part))
    copies = []
    for p in range(yx):
        copies.append((C * p, 0, 0, p, 0, 0, tall, HD))
        copies.append((C * p + 1, 0, 0, p, 0, HD, tall, 2 * HD))
        for z in range(Z):
            column = (z * yx + places_yx[p], unit)
            copies.append((C * yx, 0, column, p, tall, z * unit, row_count, unit))
        copies.append((C * yx + 1, 0, 0, p, tall, tall, row_count, span - tall))
    last_grads = shuffle(
        [part for pair in last_grads for part in pair]
        + [row_grads, jnp.zeros((row_count, span - tall), BF)],
        [(tall + row_count, span)] * yx,
        copies,
    )
    share_mid, last_grads, blocks, heads_low, d_proj_halves, down_got, down_grads = stage(
        share_mid, last_grads, blocks, heads_low, d_proj_halves, down_got, down_grads
    )
    share_next = give_to(blocks[1], "z", Z, 1)
    last_got = sum_first(last_grads, y_count)
    out_grad = both_rows((heads_low[:group_rows], heads_low[group_rows:]), d_proj_halves)
    share_next, last_got, last_grads, out_grad, blocks, down_got, down_grads = stage(
        share_next, last_got, last_grads, out_grad, blocks, down_got, down_grads
    )
    shares = [blocks[0], share_mid, share_next, give_to(blocks[3], "z", Z, 3)]
    last_got = sum_second(last_grads, list(last_got), y_count)
    out_both = order_cores(*by_core(out_grad, yx // 2), first, 0)
    grad_down = sum_total(down_grads, down_got)
    shares, last_got, last_grads, out_both, gu_arrived, ple_arrived = stage(
        shares, last_got, last_grads, out_both, gu_arrived, ple_arrived
    )
    d_normed = d_normed_own + add_up(shares)

    last_low = sum_total(last_grads, last_got).astype(BF)
    qkv_pair = by_core(last_low[:tall], Z)
    qkv_cores = [jnp.where(first, *qkv_pair), jnp.where(first, *qkv_pair[::-1])]
    heights = [min(shard, row_count - low) for low in range(0, row_count, shard)]
    copies = []
    for k in range(Z):
        z_to = (zi + k) % Z
        for c in range(C):
            copies.append((c, (z_to, shard), 0, k, 0, c * span, shard, span))
        for j, height in enumerate(heights):
            copies.append(
                (2, tall + j * shard, (z_to, unit), k, 0, C * span + j * unit, height, unit)
            )
    last_sends = shuffle(
        qkv_cores + [last_low], [(shard, C * span + len(heights) * unit)] * Z, copies
    )
    last_sends, out_both, gu_arrived, ple_arrived, d_normed = stage(
        last_sends, out_both, gu_arrived, ple_arrived, d_normed
    )
    last_arrived = z_send(lambda k: last_sends[k])
    out_grads = [
        lax.dynamic_slice_in_dim(out_both, places_yx[p] * shard, shard) for p in range(yx)
    ]
    grad_out = sum_total(out_grads, sum_second(out_grads, sum_first(out_grads, y_count), y_count))
    ple_total = own_core(sum(piece.astype(F32) for piece in ple_arrived))
    _, norm_pull = jax.vjp(rms_norm, token_vals, gains[0])
    d_tokens_norm, _ = norm_pull(d_normed)
    d_tokens = d_branch + d_tokens_norm
    copies = []
    for k in range(Z):
        for c in range(C):
            for m in range(2):
                for a in range(yx):
                    column = (((zi - k) % Z * yx + a) * C + c, ff_shard)
                    source = (k, m * ff_own) if c == 0 else ((1 + m) * Z + k, 0)
                    copies.append(
                        (
                            source[0], 0, source[1] + a * ff_shard,
                            m, 0, column, shard, ff_shard,
                        )
                    )
    grad_gu = shuffle(list(gu_arrived), [(shard, Z * yx * C * ff_shard)] * 2, copies)
    grad_gu = [grad.astype(F32) for grad in grad_gu]
    qkv_parts = z_place(last_arrived, zi)[:, : C * span].astype(F32)
    row_total = sum(piece[:, C * span :].astype(F32) for piece in last_arrived)
    row_total = jnp.concatenate(
        [row_total[:height, j * unit : (j + 1) * unit] for j, height in enumerate(heights)], axis=0
    )
    row_keep = jnp.where(first, row_total[:, :shard], row_total[:, shard:])
    row_send = jnp.where(first, row_total[:, shard:], row_total[:, :shard])
    row_total = row_keep + swap_core(row_send.astype(BF)).astype(F32)

    def qkv_part(z, c, m):
        return qkv_parts[z * shard : (z + 1) * shard, (3 * c + m) * HD : (3 * c + m + 1) * HD]

    grad_query = jnp.concatenate([qkv_part(z, c, 0) for z in range(Z) for c in range(C)], axis=1)
    grad_kv = [
        jnp.concatenate(
            [
                sum(
                    qkv_part(z, c, m)
                    for z in range(h * Z // KVH, (h + 1) * Z // KVH)
                    for c in range(C)
                )
                for h in range(KVH)
            ],
            axis=1,
        )
        for m in (1, 2)
    ]
    grad_gains = row_total[lanes : lanes + gain_count]
    grad_qk = row_total[lanes + gain_count : lanes + gain_count + 2, :qk_shard]
    return (
        output.astype(BF)[None],
        d_tokens.astype(BF)[None],
        d_extra.astype(BF)[None],
        grad_query,
        grad_kv[0],
        grad_kv[1],
        grad_out,
        row_total[:left_rank].T,
        row_total[left_rank:lanes],
        grad_gains,
        grad_qk,
        grad_gu[0],
        grad_gu[1],
        grad_down,
        ple_total[:, :ple],
        ple_total[:, ple:].T,
    )


def solution(mesh):
    fine = Mesh(mesh.devices.reshape(Z, -1, X, C), EVERY)
    rows = P(EVERY, None)
    cols = P(None, EVERY)
    stream = P(("x", "c"), ("z", "y"), None)
    return jax.shard_map(
        local,
        mesh=fine,
        in_specs=(
            stream, stream, stream, P(("x", "c"), None), P(),
            rows, rows, rows, rows, rows, cols, cols, cols, rows, rows, rows, rows, cols,
        ),
        out_specs=(
            stream, stream, stream,
            rows, rows, rows, rows, rows, cols, cols, cols, rows, rows, rows, rows, cols,
        ),
        check_vma=False,
    )
```
